256 devices in a mesh: prompt: 8 (over y, z_hi), wide: 32 (over x, z_lo, core).
Axes of the slice: x: 4, y: 4, z: 8 (z_hi: 2, z_lo: 4; z = z_hi * 4 + z_lo), core: 2. Of those that a mesh axis runs over, the one named last changes fastest.
Arguments:
- candidate_hidden: bfloat16 [8, 4096, 4096], P('prompt', 'wide'), may hold values from -6 to 6
- frozen_query: bfloat16 [8, 4096, 4096], P('prompt', 'wide'), may hold values from -12 to 12
- candidate_key_value: bfloat16 [8, 4096, 2048], P('prompt', 'wide'), may hold values from -6 to 6
- prompt_key_value: bfloat16 [8, 2048, 2048], P('prompt', 'wide'), may hold values from -12 to 12
- candidate_adapter: int32 [8, 32], P('prompt'), may hold values from 0 to 15
- prompt_block_end: int32 [8, 32], P('prompt', 'wide'), may hold values from 1 to 16, as said below
- adapter_down: bfloat16 [16, 4, 16, 4096], P(None, None, None, 'wide'), may hold values from -0.09375 to 0.09375
- adapter_up: bfloat16 [16, 2, 16, 4096], P(None, None, None, 'wide'), may hold values from -0.625 to 0.625
- adapter_up_key_value: bfloat16 [16, 2, 16, 1024], P(None, None, None, 'wide'), may hold values from -0.625 to 0.625
- output_cotangent: bfloat16 [8, 4096, 4096], P('prompt', 'wide'), may hold values from -0.03125 to 0.03125
- context_cotangent: bfloat16 [8, 4096, 4096], P('prompt', 'wide'), may hold values from -0.03125 to 0.03125
Outputs:
- down_gradient: float32 [16, 4, 16, 4096], P(None, None, None, 'wide')
- up_gradient: float32 [16, 2, 16, 4096], P(None, None, None, 'wide')
- key_value_up_gradient: float32 [16, 2, 16, 1024], P(None, None, None, 'wide')
The draws below stay inside these ranges and needn't reach their ends.
Inputs may be any that keep to these rules, and one draw needn't show every extreme that they name: `prompt_block_end`: the first block of every group sees the whole prompt.
All inputs are finite; a program needn't handle non-finite values.
Results may differ from the reference program's by a relative error of at most 0.02.
Values may be sent and summed in bfloat16 or wider, within the bound.
No kernel may reach another device: no remote copies, remote signals or barrier semaphores. Data moves between devices by JAX's collectives and lax.ppermute only.
A program may use at most 192 MiB of HBM per device.

```python
import jax
import jax.numpy as jnp
from jax import lax

MODEL_WIDTH = 4096
HEADS = 32
KV_HEADS = 8
HEAD_DIM = 128
ADAPTER_RANK = 16
ADAPTER_COUNT = 16
BLOCK_TOKENS = 128
KEY_VALUE_WIDTH = 1024
GROUPS = 8
CBLK = 32
CROWS = 4096
PROMPT_LEN = 2048
PBLOCKS = 16


def draw_prompt_key_value(key, part):
    noise = jnp.clip(jax.random.normal(jax.random.fold_in(key, 11), (GROUPS, PROMPT_LEN, 2 * KV_HEADS * HEAD_DIM), jnp.float32), -6.0, 6.0)
    return noise.astype(jnp.bfloat16)


def draw_frozen_query(key, part):
    noise = jnp.clip(jax.random.normal(jax.random.fold_in(key, 21), (GROUPS, CROWS, HEADS * HEAD_DIM), jnp.float32), -6.0, 6.0)
    return noise.astype(jnp.bfloat16)


def draw_prompt_block_end(key, part):
    ends = jax.random.randint(jax.random.fold_in(key, 31), (GROUPS, CBLK), 1, PBLOCKS + 1)
    return ends.at[:, 0].set(PBLOCKS).astype(jnp.int32)


def place_ends(values, key, low, top_value):
    dims = values.shape
    spot = [jax.random.randint(jax.random.fold_in(key, axis), (), 0, dims[axis]) for axis in range(len(dims))]
    values = values.at[tuple(spot)].set(low)
    longest = dims.index(max(dims))
    spot[longest] = (spot[longest] + 1) % dims[longest]
    return values.at[tuple(spot)].set(top_value)


def steps_of(key, shape, pieces, smallest, high):
    factor_of, own = 1.0, jax.random.fold_in(key, 6)
    for position, shards_of in pieces:
        heights = jnp.exp(jax.random.uniform(jax.random.fold_in(own, position), (shards_of,), jnp.float32, smallest / len(pieces), high / len(pieces)))
        factor_of = factor_of * jnp.repeat(heights, shape[position] // shards_of).reshape([-1 if axis == position else 1 for axis in range(len(shape))])
    return factor_of


def centred(rng, shape, width, reach, split=(), held_as=jnp.bfloat16):
    values = width * jax.random.normal(rng, shape, jnp.float32)
    if split:
        values = values * steps_of(rng, shape, split, -0.22, 0.18)
    return jnp.clip(values, -reach, reach).astype(held_as)


def setup_inputs(seed: int = 0) -> dict:
    arg_keys = jax.random.split(jax.random.key(seed), 12)
    return {
        "candidate_hidden": centred(arg_keys[0], (GROUPS, CROWS, MODEL_WIDTH), 1.0, 6.0, ((0, 8), (1, 32))),
        "frozen_query": draw_frozen_query(jax.random.fold_in(arg_keys[11], 71), 0),
        "candidate_key_value": centred(arg_keys[2], (GROUPS, CROWS, 2 * KEY_VALUE_WIDTH), 1.0, 6.0, ((0, 8), (1, 32))),
        "prompt_key_value": draw_prompt_key_value(jax.random.fold_in(arg_keys[11], 71), 0),
        "candidate_adapter": place_ends(jax.random.randint(arg_keys[4], (GROUPS, CBLK), 0, ADAPTER_COUNT), jax.random.fold_in(arg_keys[4], 1), 0, ADAPTER_COUNT - 1).astype(jnp.int32),
        "prompt_block_end": draw_prompt_block_end(jax.random.fold_in(arg_keys[11], 71), 0),
        "adapter_down": centred(arg_keys[6], (ADAPTER_COUNT, 4, ADAPTER_RANK, MODEL_WIDTH), MODEL_WIDTH ** -0.5, 0.09375, ((3, 32),)),
        "adapter_up": centred(arg_keys[7], (ADAPTER_COUNT, 2, ADAPTER_RANK, MODEL_WIDTH), 0.1, 0.625, ((3, 32),)),
        "adapter_up_key_value": centred(arg_keys[8], (ADAPTER_COUNT, 2, ADAPTER_RANK, KEY_VALUE_WIDTH), 0.1, 0.625, ((3, 32),)),
        "output_cotangent": centred(arg_keys[9], (GROUPS, CROWS, MODEL_WIDTH), 0.005, 0.03125, ((0, 8), (1, 32))),
        "context_cotangent": centred(arg_keys[10], (GROUPS, CROWS, MODEL_WIDTH), 0.005, 0.03125, ((0, 8), (1, 32))),
    }


adapter_scale = 2.0
masked_score = -1.0e30


def rounded_input(value):
    return lax.optimization_barrier(value.astype(jnp.bfloat16)).astype(jnp.float32)


def split_heads(rows):
    return rows.reshape(rows.shape[0], KV_HEADS, HEADS // KV_HEADS, HEAD_DIM)


def per_block_gradients(hidden_rows, candidate_query_rows, key_value_rows, output_gradients, context_gradients, adapter_index, last_prompt_block, prompt_token_rows, adapter_down, adapter_up, adapter_up_key_value):
    key_value_width = KV_HEADS * HEAD_DIM
    inverse_root = HEAD_DIM ** -0.5
    down_matrices = adapter_down[adapter_index].astype(jnp.float32)
    up_model_matrix = adapter_up[adapter_index].astype(jnp.float32)
    up_matrix_pairs = adapter_up_key_value[adapter_index].astype(jnp.float32)
    x_wide = hidden_rows.astype(jnp.float32)
    rank_projection = rounded_input(jnp.einsum('bd,prd->prb', x_wide, down_matrices[:3]))
    query_vectors = rounded_input(candidate_query_rows.astype(jnp.float32) + adapter_scale * jnp.einsum('hc,hp->cp', rank_projection[0], up_model_matrix[0]))
    key_value_delta = jnp.einsum('prb,prd->bpd', rank_projection[1:], up_matrix_pairs).reshape(BLOCK_TOKENS, 2 * key_value_width)
    candidate_own_key_value = rounded_input(key_value_rows.astype(jnp.float32) + adapter_scale * key_value_delta)
    prompt_wide = prompt_token_rows.astype(jnp.float32)
    key_rows = jnp.concatenate([prompt_wide[:, :key_value_width], candidate_own_key_value[:, :key_value_width]], axis=0)
    value_rows = jnp.concatenate([prompt_wide[:, key_value_width:], candidate_own_key_value[:, key_value_width:]], axis=0)
    prompt_len = prompt_token_rows.shape[0]
    prompt_seen = jnp.arange(prompt_len)[None, :] < last_prompt_block * BLOCK_TOKENS
    causal = jnp.arange(BLOCK_TOKENS)[None, :] <= jnp.arange(BLOCK_TOKENS)[:, None]
    visible = jnp.concatenate([jnp.broadcast_to(prompt_seen, (BLOCK_TOKENS, prompt_len)), causal], axis=1)
    query_heads = split_heads(query_vectors)
    key_heads = key_rows.reshape(-1, KV_HEADS, HEAD_DIM)
    value_heads = value_rows.reshape(-1, KV_HEADS, HEAD_DIM)
    scores = jnp.where(visible, jnp.einsum('bkgd,jkd->kgbj', query_heads, key_heads) * inverse_root, masked_score)
    row_peak = jnp.max(scores, axis=-1, keepdims=True)
    exponent = jnp.where(visible, jnp.exp(scores - row_peak), 0.0)
    row_total = jnp.sum(exponent, axis=-1)
    weighted = jnp.einsum('kgbj,jkd->bkgd', rounded_input(exponent), value_heads)
    context = rounded_input(weighted / jnp.transpose(row_total, (2, 0, 1))[..., None]).reshape(BLOCK_TOKENS, HEADS * HEAD_DIM)
    output_model_rows = output_gradients.astype(jnp.float32)
    output_rank_rows = rounded_input(jnp.einsum('ae,me->ma', context, down_matrices[3]))
    up_gradient_result = adapter_scale * jnp.einsum('su,ui->si', output_rank_rows, output_model_rows)
    up_output_matrix = rounded_input(adapter_scale * jnp.einsum('ae,me->ma', output_model_rows, up_model_matrix[1]))
    grad_a_out = jnp.einsum('su,ui->si', up_output_matrix, context)
    context_grad = rounded_input(context_gradients.astype(jnp.float32) + jnp.einsum('hc,hp->cp', up_output_matrix, down_matrices[3]))
    grad_heads = split_heads(context_grad)
    row_delta = jnp.transpose(jnp.sum(grad_heads * split_heads(context), axis=-1), (1, 2, 0))
    attention = exponent / row_total[..., None]
    attention_grad = jnp.einsum('bkgd,jkd->kgbj', grad_heads, value_heads)
    score_grad = rounded_input(attention * (attention_grad - row_delta[..., None]))
    query_gradient = rounded_input(jnp.einsum('kgbj,jkd->bkgd', score_grad, key_heads) * inverse_root).reshape(BLOCK_TOKENS, HEADS * HEAD_DIM)
    key_grad = jnp.einsum('kgbj,bkgd->jkd', score_grad[..., prompt_len:], query_heads) * inverse_root
    value_grad = jnp.einsum('kgbj,bkgd->jkd', rounded_input(attention[..., prompt_len:]), grad_heads)
    key_value_gradient = rounded_input(jnp.stack([key_grad.reshape(BLOCK_TOKENS, key_value_width), value_grad.reshape(BLOCK_TOKENS, key_value_width)], axis=1))
    up_query_matrix = rounded_input(adapter_scale * jnp.einsum('ae,me->ma', query_gradient, up_model_matrix[0]))
    up_rank_key_value = rounded_input(adapter_scale * jnp.einsum('ztf,tkf->tkz', key_value_gradient, up_matrix_pairs))
    grad_a_qkv = jnp.einsum('prb,bd->prd', jnp.concatenate([up_query_matrix[None], up_rank_key_value], axis=0), x_wide)
    down_gradient = jnp.concatenate([grad_a_qkv, grad_a_out[None]], axis=0)
    up_gradient = jnp.stack([adapter_scale * jnp.einsum('su,ui->si', rank_projection[0], query_gradient), up_gradient_result], axis=0)
    key_value_up_gradient = adapter_scale * jnp.einsum('yzm,myk->yzk', rank_projection[1:], key_value_gradient)
    return down_gradient, up_gradient, key_value_up_gradient


def reference(candidate_hidden, frozen_query, candidate_key_value, prompt_key_value, candidate_adapter, prompt_block_end, adapter_down, adapter_up, adapter_up_key_value, output_cotangent, context_cotangent):
    block_count = GROUPS * CBLK
    block_items = (
        candidate_hidden.reshape(block_count, BLOCK_TOKENS, -1),
        frozen_query.reshape(block_count, BLOCK_TOKENS, -1),
        candidate_key_value.reshape(block_count, BLOCK_TOKENS, -1),
        output_cotangent.reshape(block_count, BLOCK_TOKENS, -1),
        context_cotangent.reshape(block_count, BLOCK_TOKENS, -1),
        candidate_adapter.reshape(block_count).astype(jnp.int32),
        prompt_block_end.reshape(block_count).astype(jnp.int32),
        (jnp.arange(block_count) // CBLK).astype(jnp.int32),
    )

    def accumulate(running, item_now):
        hidden_rows, candidate_query_rows, key_value_rows, output_gradients, context_gradients, adapter_index, last_prompt_block, group_index = item_now
        prompt_token_rows = lax.dynamic_index_in_dim(prompt_key_value, group_index, 0, keepdims=False)
        down_gradient, up_gradient, key_value_up_gradient = per_block_gradients(hidden_rows, candidate_query_rows, key_value_rows, output_gradients, context_gradients, adapter_index, last_prompt_block, prompt_token_rows, adapter_down, adapter_up, adapter_up_key_value)
        return (running[0].at[adapter_index].add(down_gradient), running[1].at[adapter_index].add(up_gradient), running[2].at[adapter_index].add(key_value_up_gradient)), None

    start_state = (
        jnp.zeros(adapter_down.shape, jnp.float32),
        jnp.zeros(adapter_up.shape, jnp.float32),
        jnp.zeros(adapter_up_key_value.shape, jnp.float32),
    )
    totals, _ = lax.scan(accumulate, start_state, block_items)
    return totals[0], totals[1], totals[2]
```

```python
import functools

import jax
import jax.numpy as jnp
from jax import lax
from jax.experimental import pallas as pl
from jax.experimental.pallas import tpu as pltpu
from jax.sharding import PartitionSpec as P

HEADS = 32
KV_HEADS = 8
HEAD_DIM = 128
ADAPTERS = 16
RANK = 16
BLOCK = 128
WIDE = 32
ROWS = 104
ADAPTER_SCALE = 2.0
MASKED = -1e30
INVERSE_ROOT = HEAD_DIM ** (-0.5)
LOG2E = 1.4426950408889634
KEY_CHUNK = 256

BF16 = jnp.bfloat16
F32 = jnp.float32


def dot(a, b, dims):
    return lax.dot_general(a, b, (dims, ((), ())), preferred_element_type=F32)


NN = ((1,), (0,))
NT = ((1,), (1,))
TN = ((0,), (0,))


def vmem(n):
    return [pl.BlockSpec(memory_space=pltpu.VMEM)] * n


def smem():
    return pl.BlockSpec(memory_space=pltpu.SMEM)


def pack_kernel(ids_ref, down_ref, up_ref, pair_ref, out_ref):
    def step(n, carry):
        a = ids_ref[0, n]
        for p in range(4):
            out_ref[n, 16 * p : 16 * p + 16, :] = down_ref[a, p]
        for p in range(2):
            out_ref[n, 64 + 16 * p : 80 + 16 * p, :] = up_ref[a, p]
        pieces = []
        for p in range(2):
            pair = pair_ref[a, p].astype(F32)
            pieces += [pair[:8], pair[8:]]
        out_ref[n, 96:104, :] = jnp.concatenate(pieces, axis=1).astype(BF16)
        return carry

    lax.fori_loop(0, WIDE, step, 0)


def pack(ids, down, up, pairs):
    return pl.pallas_call(
        pack_kernel,
        out_shape=jax.ShapeDtypeStruct((WIDE, ROWS, 128), BF16),
        in_specs=[smem()] + vmem(3),
        out_specs=pl.BlockSpec(memory_space=pltpu.VMEM),
        name="pack",
    )(ids, down, up, pairs)


def wide_rows(ref, start, stop):
    return jnp.concatenate([ref[s, start:stop, :] for s in range(WIDE)], axis=1)


def pair_rows(ref):
    parts = []
    for g in range(4):
        pieces = []
        for s in range(WIDE):
            pieces.append(ref[s, 96:104, 32 * g : 32 * g + 32].astype(F32))
        parts.append(jnp.concatenate(pieces, axis=1))
    return jnp.concatenate(parts, axis=0).astype(BF16)


def prep_kernel(
    mine_ref, x_ref, fq_ref, ckv_ref, oc_ref, cc_ref,
    q_ref, own_ref, cg_ref, low_ref, upout_ref, pair_ref,
):
    low = dot(wide_rows(mine_ref, 0, 48), x_ref[0], NT).astype(BF16)
    low_ref[...] = low
    up_out = (ADAPTER_SCALE * dot(wide_rows(mine_ref, 80, 96), oc_ref[0], NT)).astype(BF16)
    upout_ref[...] = up_out
    pairs = pair_rows(mine_ref)
    pair_ref[...] = pairs
    for s in range(WIDE):
        cols = slice(128 * s, 128 * s + 128)
        delta = dot(low[:16], mine_ref[s, 64:80, :], TN)
        q_ref[:, cols] = (fq_ref[0, :, cols].astype(F32) + ADAPTER_SCALE * delta).astype(BF16)
        delta = dot(up_out, mine_ref[s, 48:64, :], TN)
        cg_ref[:, cols] = (cc_ref[0, :, cols].astype(F32) + delta).astype(BF16)
    for h in range(2):
        cols = slice(1024 * h, 1024 * h + 1024)
        delta = dot(low[16 + 16 * h : 32 + 16 * h], pairs[16 * h : 16 * h + 16], TN)
        own_ref[:, cols] = (ckv_ref[0, :, cols].astype(F32) + ADAPTER_SCALE * delta).astype(BF16)


def prep(mine, x, fq, ckv, oc, cc):
    return pl.pallas_call(
        prep_kernel,
        out_shape=(
            jax.ShapeDtypeStruct((BLOCK, 4096), BF16),
            jax.ShapeDtypeStruct((BLOCK, 2048), BF16),
            jax.ShapeDtypeStruct((BLOCK, 4096), BF16),
            jax.ShapeDtypeStruct((48, 128), BF16),
            jax.ShapeDtypeStruct((16, 128), BF16),
            jax.ShapeDtypeStruct((32, 1024), BF16),
        ),
        in_specs=vmem(6),
        out_specs=tuple(vmem(6)),
        name="prep",
    )(mine, x, fq, ckv, oc, cc)


def stack_heads(ref):
    return jnp.concatenate([ref[:, 128 * g : 128 * g + 128] for g in range(4)], axis=0)


def attention_kernel(
    end_ref, q_ref, cg_ref, k_ref, v_ref, ok_ref, ov_ref,
    ctx_ref, dq_ref, dk_ref, dv_ref, s_ref, p_ref,
):
    keys = k_ref.shape[0]
    chunks = keys // KEY_CHUNK
    factor = INVERSE_ROOT * LOG2E
    limit = end_ref[0, 0] * BLOCK
    q4 = stack_heads(q_ref)
    cg4 = stack_heads(cg_ref)
    own_k = ok_ref[...]
    own_v = ov_ref[...]
    row = lax.broadcasted_iota(jnp.int32, (512, BLOCK), 0) & (BLOCK - 1)
    col = lax.broadcasted_iota(jnp.int32, (512, BLOCK), 1)
    own_s = jnp.where(col <= row, dot(q4, own_k, NT), MASKED)
    peak = own_s
    for j in range(chunks):
        rows = slice(KEY_CHUNK * j, KEY_CHUNK * (j + 1))
        s = dot(q4, k_ref[rows, :], NT)
        position = lax.broadcasted_iota(jnp.int32, (1, KEY_CHUNK), 1) + KEY_CHUNK * j
        s = jnp.where(position < limit, s, MASKED)
        s_ref[:, rows] = s
        for t in range(KEY_CHUNK // 128):
            peak = jnp.maximum(peak, s[:, 128 * t : 128 * t + 128])
    peak = jnp.max(peak, axis=1, keepdims=True) * factor
    own_p = jnp.exp2(own_s * factor - peak)
    total = own_p
    weighted = dot(own_p.astype(BF16), own_v, NN)
    for j in range(chunks):
        rows = slice(KEY_CHUNK * j, KEY_CHUNK * (j + 1))
        p = jnp.exp2(s_ref[:, rows] * factor - peak)
        for t in range(KEY_CHUNK // 128):
            total = total + p[:, 128 * t : 128 * t + 128]
        p16 = p.astype(BF16)
        p_ref[:, rows] = p16
        weighted = weighted + dot(p16, v_ref[rows, :], NN)
    total = jnp.sum(total, axis=1, keepdims=True)
    context = (weighted / total).astype(BF16)
    delta = jnp.sum(cg4.astype(F32) * context.astype(F32), axis=1, keepdims=True)
    attention = own_p / total
    own_ds = (attention * (dot(cg4, own_v, NT) - delta)).astype(BF16)
    grad = jnp.zeros((512, 128), F32)
    for j in range(chunks):
        rows = slice(KEY_CHUNK * j, KEY_CHUNK * (j + 1))
        dp = dot(cg4, v_ref[rows, :], NT)
        ds = (p_ref[:, rows].astype(F32) * (dp - delta)).astype(BF16)
        grad = grad + dot(ds, k_ref[rows, :], NN)
    grad = (grad / total + dot(own_ds, own_k, NN)) * INVERSE_ROOT
    grad = grad.astype(BF16)
    for g in range(4):
        ctx_ref[:, 128 * g : 128 * g + 128] = context[128 * g : 128 * g + 128]
        dq_ref[:, 128 * g : 128 * g + 128] = grad[128 * g : 128 * g + 128]
    dk_ref[...] = (dot(own_ds, q4, TN) * INVERSE_ROOT).astype(BF16)
    dv_ref[...] = dot(attention.astype(BF16), cg4, TN).astype(BF16)


def attention_call(end, q, cg, kv, own):
    keys = kv.shape[0]
    heads = pl.BlockSpec((BLOCK, 512), lambda k: (0, k))
    head = pl.BlockSpec((BLOCK, 128), lambda k: (0, k))
    return pl.pallas_call(
        attention_kernel,
        grid=(KV_HEADS,),
        out_shape=(
            jax.ShapeDtypeStruct((BLOCK, 4096), BF16),
            jax.ShapeDtypeStruct((BLOCK, 4096), BF16),
            jax.ShapeDtypeStruct((BLOCK, 1024), BF16),
            jax.ShapeDtypeStruct((BLOCK, 1024), BF16),
        ),
        in_specs=[
            smem(),
            heads,
            heads,
            pl.BlockSpec((keys, 128), lambda k: (0, k)),
            pl.BlockSpec((keys, 128), lambda k: (0, k + KV_HEADS)),
            head,
            pl.BlockSpec((BLOCK, 128), lambda k: (0, k + KV_HEADS)),
        ],
        out_specs=(heads, heads, head, head),
        scratch_shapes=[
            pltpu.VMEM((512, keys), F32),
            pltpu.VMEM((512, keys), BF16),
        ],
        compiler_params=pltpu.CompilerParams(dimension_semantics=("arbitrary",)),
        name="attend",
    )(end, q, cg, kv, kv, own, own)


def grads_kernel(
    mine_ref, x_ref, oc_ref, low_ref, upout_ref, pair_ref,
    ctx_ref, dq_ref, dk_ref, dv_ref, out_ref,
):
    low = low_ref[...]
    context = ctx_ref[...]
    dq = dq_ref[...]
    dk = dk_ref[...]
    dv = dv_ref[...]
    out_low = dot(wide_rows(mine_ref, 48, 64), context, NT).astype(BF16)
    up_q = (ADAPTER_SCALE * dot(wide_rows(mine_ref, 64, 80), dq, NT)).astype(BF16)
    up_k = (ADAPTER_SCALE * dot(pair_ref[:16], dk, NT)).astype(BF16)
    up_v = (ADAPTER_SCALE * dot(pair_ref[16:], dv, NT)).astype(BF16)
    up_low = jnp.concatenate([up_q, up_k, up_v], axis=0)
    up_out = upout_ref[...]
    for s in range(WIDE):
        cols = slice(128 * s, 128 * s + 128)
        out_ref[s, 0:48, :] = dot(up_low, x_ref[0, :, cols], NN).astype(BF16)
        out_ref[s, 48:64, :] = dot(up_out, context[:, cols], NN).astype(BF16)
        out_ref[s, 64:80, :] = (ADAPTER_SCALE * dot(low[:16], dq[:, cols], NN)).astype(BF16)
        out_ref[s, 80:96, :] = (ADAPTER_SCALE * dot(out_low, oc_ref[0, :, cols], NN)).astype(BF16)
    pairs = [
        ADAPTER_SCALE * dot(low[16:32], dk, NN),
        ADAPTER_SCALE * dot(low[32:48], dv, NN),
    ]
    for s in range(WIDE):
        cols = slice(32 * s, 32 * s + 32)
        out_ref[s, 96:104, :] = jnp.concatenate(
            [pairs[0][:8, cols], pairs[0][8:, cols], pairs[1][:8, cols], pairs[1][8:, cols]], axis=1
        ).astype(BF16)


def grads(mine, x, oc, low, up_out, pairs, context, dq, dk, dv):
    return pl.pallas_call(
        grads_kernel,
        out_shape=jax.ShapeDtypeStruct((WIDE, ROWS, 128), BF16),
        in_specs=vmem(10),
        out_specs=pl.BlockSpec(memory_space=pltpu.VMEM),
        name="grads",
    )(mine, x, oc, low, up_out, pairs, context, dq, dk, dv)


def combine_kernel(ids_ref, lane_ref, back_ref, mine_ref, o1_ref, o2_ref, o3_ref, acc_ref):
    acc_ref[...] = jnp.zeros_like(acc_ref)

    def step(n, carry):
        a = ids_ref[0, n]
        acc_ref[a] += back_ref[n].astype(F32)
        return carry

    lax.fori_loop(0, WIDE, step, 0)
    y = lane_ref[0]
    mine_ref[...] = acc_ref[pl.ds(4 * y, 4)]
    for shift, ref in ((1, o1_ref), (2, o2_ref), (3, o3_ref)):
        ref[...] = acc_ref[pl.ds(4 * lax.rem(y + shift, 4), 4)].astype(BF16)


def combine(ids, place, back):
    quarter = (4, ROWS, 128)
    return pl.pallas_call(
        combine_kernel,
        out_shape=(
            jax.ShapeDtypeStruct(quarter, F32),
            jax.ShapeDtypeStruct(quarter, BF16),
            jax.ShapeDtypeStruct(quarter, BF16),
            jax.ShapeDtypeStruct(quarter, BF16),
        ),
        in_specs=[smem(), smem()] + vmem(1),
        out_specs=tuple(vmem(4)),
        scratch_shapes=[pltpu.VMEM((ADAPTERS, ROWS, 128), F32)],
        name="combine",
    )(ids, place, back)


def quarter_kernel(lane_ref, mine_ref, r1_ref, r2_ref, r3_ref, keep_ref, send_ref):
    z = lane_ref[1]
    for t in range(2):
        for out, start in ((keep_ref, 2 * z), (send_ref, 2 - 2 * z)):
            value = mine_ref[start + t]
            for ref in (r1_ref, r2_ref, r3_ref):
                value = value + ref[start + t].astype(F32)
            out[t] = value.astype(out.dtype)


def quarter_sum(place, mine, received):
    half = (2, ROWS, 128)
    return pl.pallas_call(
        quarter_kernel,
        out_shape=(jax.ShapeDtypeStruct(half, F32), jax.ShapeDtypeStruct(half, BF16)),
        in_specs=[smem()] + vmem(4),
        out_specs=tuple(vmem(2)),
        name="quarter",
    )(place, mine, *received)


def add_kernel(a_ref, b_ref, out_ref):
    out_ref[...] = (a_ref[...] + b_ref[...].astype(F32)).astype(BF16)


def add_half(a, b):
    return pl.pallas_call(
        add_kernel,
        out_shape=jax.ShapeDtypeStruct(a.shape, BF16),
        in_specs=vmem(2),
        out_specs=pl.BlockSpec(memory_space=pltpu.VMEM),
        name="halfsum",
    )(a, b)


def join_kernel(lane_ref, a_ref, b_ref, out_ref):
    z = lane_ref[1]
    out_ref[pl.ds(2 * z, 2)] = a_ref[...]
    out_ref[pl.ds(2 - 2 * z, 2)] = b_ref[...]


def join(place, a, b):
    return pl.pallas_call(
        join_kernel,
        out_shape=jax.ShapeDtypeStruct((4, ROWS, 128), BF16),
        in_specs=[smem()] + vmem(2),
        out_specs=pl.BlockSpec(memory_space=pltpu.VMEM),
        name="joined",
    )(place, a, b)


def unpack_kernel(lane_ref, q0_ref, q1_ref, q2_ref, q3_ref, down_ref, up_ref, pair_ref):
    y = lane_ref[0]
    for shift, ref in ((0, q0_ref), (1, q1_ref), (2, q2_ref), (3, q3_ref)):
        first = 4 * lax.rem(y + 4 - shift, 4)
        for t in range(4):
            a = first + t
            value = ref[t].astype(F32)
            for p in range(4):
                down_ref[a, p] = value[16 * p : 16 * p + 16]
            for p in range(2):
                up_ref[a, p] = value[64 + 16 * p : 80 + 16 * p]
                for h in range(2):
                    g = 2 * p + h
                    pair_ref[a, p, 8 * h : 8 * h + 8, :] = value[96:104, 32 * g : 32 * g + 32]


def unpack(place, quarters):
    return pl.pallas_call(
        unpack_kernel,
        out_shape=(
            jax.ShapeDtypeStruct((ADAPTERS, 4, RANK, 128), F32),
            jax.ShapeDtypeStruct((ADAPTERS, 2, RANK, 128), F32),
            jax.ShapeDtypeStruct((ADAPTERS, 2, RANK, 32), F32),
        ),
        in_specs=[smem()] + vmem(4),
        out_specs=tuple(vmem(3)),
        name="unpack",
    )(place, *quarters)


def y_shift(value, shift):
    pairs = [(2 * y + z, 2 * ((y + shift) % 4) + z) for y in range(4) for z in range(2)]
    return lax.ppermute(value, "prompt", pairs)


def z_swap(value):
    return lax.ppermute(value, "prompt", [(p, p ^ 1) for p in range(8)])


def body(
    candidate_hidden, frozen_query, candidate_key_value, prompt_key_value, candidate_adapter,
    prompt_block_end, adapter_down, adapter_up, adapter_up_key_value, output_cotangent,
    context_cotangent,
):
    group = lax.axis_index("prompt")
    place = jnp.stack([group // 2, group % 2]).astype(jnp.int32)
    gathered = lax.all_gather(prompt_key_value[0], "wide", axis=0, tiled=True)
    sent = pack(candidate_adapter, adapter_down, adapter_up, adapter_up_key_value)
    mine = lax.all_to_all(sent, "wide", 0, 0, tiled=True)
    q, own, cg, low, up_out, pairs = prep(
        mine, candidate_hidden, frozen_query, candidate_key_value, output_cotangent,
        context_cotangent,
    )
    context, dq, dk, dv = attention_call(prompt_block_end, q, cg, gathered, own)
    blocks = grads(mine, candidate_hidden, output_cotangent, low, up_out, pairs, context, dq, dk, dv)
    back = lax.all_to_all(blocks, "wide", 0, 0, tiled=True)
    total, *others = combine(candidate_adapter, place, back)
    received = [y_shift(other, shift) for shift, other in zip((1, 2, 3), others)]
    keep, send = quarter_sum(place, total, received)
    half = add_half(keep, z_swap(send))
    quarter = join(place, half, z_swap(half))
    quarters = [quarter] + [y_shift(quarter, shift) for shift in (1, 2, 3)]
    return unpack(place, quarters)


def solution(mesh):
    tokens = P("prompt", "wide", None)
    columns = P(None, None, None, "wide")
    placed = (
        tokens, tokens, tokens, tokens, P("prompt", None), P("prompt", "wide"),
        columns, columns, columns, tokens, tokens,
    )
    return jax.shard_map(
        body, mesh=mesh, in_specs=placed, out_specs=(columns, columns, columns), check_vma=False
    )
```

```python
import jax
import jax.numpy as jnp
from jax import lax
from jax.experimental import pallas as pl
from jax.experimental.pallas import tpu as pltpu
from jax.sharding import PartitionSpec as P


KV_HEADS = 8
HEAD_DIM = 128
ADAPTERS = 16
RANK = 16
BLOCK = 128
WIDE = 32
ROWS = 104
ADAPTER_SCALE = 2.0
MASKED = -1e30
INVERSE_ROOT = HEAD_DIM ** (-0.5)
LOG2E = 1.4426950408889634
KEY_CHUNK = 256
SHIFTS = (0, 1, 3, 2)

BF16 = jnp.bfloat16
F32 = jnp.float32


def dot(a, b, dims):
    return lax.dot_general(a, b, (dims, ((), ())), preferred_element_type=F32)


NN = ((1,), (0,))
NT = ((1,), (1,))
TN = ((0,), (0,))


def vmem(n):
    return [pl.BlockSpec(memory_space=pltpu.VMEM)] * n


def smem():
    return pl.BlockSpec(memory_space=pltpu.SMEM)


def pack_kernel(ids_ref, down_ref, up_ref, pair_ref, out_ref):
    def step(n, carry):
        a = ids_ref[0, n]
        for p in range(4):
            out_ref[n, 16 * p : 16 * p + 16, :] = down_ref[a, p]
        for p in range(2):
            out_ref[n, 64 + 16 * p : 80 + 16 * p, :] = up_ref[a, p]
        pieces = []
        for p in range(2):
            pair = pair_ref[a, p].astype(F32)
            pieces += [pair[:8], pair[8:]]
        out_ref[n, 96:104, :] = jnp.concatenate(pieces, axis=1).astype(BF16)
        return carry

    lax.fori_loop(0, WIDE, step, 0)


def pack(ids, down, up, pairs):
    return pl.pallas_call(
        pack_kernel,
        out_shape=jax.ShapeDtypeStruct((WIDE, ROWS, 128), BF16),
        in_specs=[smem()] + vmem(3),
        out_specs=pl.BlockSpec(memory_space=pltpu.VMEM),
        compiler_params=pltpu.CompilerParams(vmem_limit_bytes=4 << 20),
        name="pack",
    )(ids, down, up, pairs)


def wide_rows(ref, start, stop):
    return jnp.concatenate([ref[s, start:stop, :] for s in range(WIDE)], axis=1)


def pair_rows(ref):
    parts = []
    for g in range(4):
        pieces = []
        for s in range(WIDE):
            pieces.append(ref[s, 96:104, 32 * g : 32 * g + 32].astype(F32))
        parts.append(jnp.concatenate(pieces, axis=1))
    return jnp.concatenate(parts, axis=0).astype(BF16)


def prep_kernel(
    mine_ref, x_ref, fq_ref, ckv_ref, oc_ref, cc_ref,
    q_ref, own_ref, cg_ref, low_ref, upout_ref, pair_ref,
):
    low = dot(wide_rows(mine_ref, 0, 48), x_ref[0], NT).astype(BF16)
    low_ref[...] = low
    up_out = (ADAPTER_SCALE * dot(wide_rows(mine_ref, 80, 96), oc_ref[0], NT)).astype(BF16)
    upout_ref[...] = up_out
    pairs = pair_rows(mine_ref)
    pair_ref[...] = pairs
    for s in range(WIDE):
        cols = slice(128 * s, 128 * s + 128)
        delta = dot(low[:16], mine_ref[s, 64:80, :], TN)
        q_ref[:, cols] = (fq_ref[0, :, cols].astype(F32) + ADAPTER_SCALE * delta).astype(BF16)
        delta = dot(up_out, mine_ref[s, 48:64, :], TN)
        cg_ref[:, cols] = (cc_ref[0, :, cols].astype(F32) + delta).astype(BF16)
    for h in range(2):
        cols = slice(1024 * h, 1024 * h + 1024)
        delta = dot(low[16 + 16 * h : 32 + 16 * h], pairs[16 * h : 16 * h + 16], TN)
        own_ref[:, cols] = (ckv_ref[0, :, cols].astype(F32) + ADAPTER_SCALE * delta).astype(BF16)


def prep(mine, x, fq, ckv, oc, cc):
    return pl.pallas_call(
        prep_kernel,
        out_shape=(
            jax.ShapeDtypeStruct((BLOCK, 4096), BF16),
            jax.ShapeDtypeStruct((BLOCK, 2048), BF16),
            jax.ShapeDtypeStruct((BLOCK, 4096), BF16),
            jax.ShapeDtypeStruct((48, 128), BF16),
            jax.ShapeDtypeStruct((16, 128), BF16),
            jax.ShapeDtypeStruct((32, 1024), BF16),
        ),
        in_specs=vmem(6),
        out_specs=tuple(vmem(6)),
        compiler_params=pltpu.CompilerParams(vmem_limit_bytes=28 << 20),
        name="prep",
    )(mine, x, fq, ckv, oc, cc)


def stack_heads(ref):
    return jnp.concatenate([ref[:, 128 * g : 128 * g + 128] for g in range(4)], axis=0)


def piece_mask(limit_ref, shift, other):
    x, z, core, end = (limit_ref[i] for i in range(4))
    side = core ^ other
    lane = lax.broadcasted_iota(jnp.int32, (1, KEY_CHUNK), 1)
    origin = jnp.zeros((1, KEY_CHUNK), jnp.int32)
    for t in range(4):
        source = (lax.rem(x + 4 - shift, 4) * 4 + lax.rem(z + 4 - t, 4)) * 2 + side
        origin = jnp.where(lane >= 64 * t, source, origin)
    return origin < 2 * end


def attention_kernel(
    limit_ref, q_ref, cg_ref, ok_ref, ov_ref, *refs,
):
    k_refs, v_refs = refs[:8], refs[8:16]
    ctx_ref, dq_ref, dk_ref, dv_ref, s_ref, p_ref = refs[16:]
    factor = INVERSE_ROOT * LOG2E
    q4 = stack_heads(q_ref)
    cg4 = stack_heads(cg_ref)
    own_k = ok_ref[...]
    own_v = ov_ref[...]
    row = lax.broadcasted_iota(jnp.int32, (512, BLOCK), 0) & (BLOCK - 1)
    col = lax.broadcasted_iota(jnp.int32, (512, BLOCK), 1)
    own_s = jnp.where(col <= row, dot(q4, own_k, NT), MASKED)
    peak = own_s
    for j in range(8):
        rows = slice(KEY_CHUNK * j, KEY_CHUNK * (j + 1))
        s = dot(q4, k_refs[j][...].reshape(KEY_CHUNK, 128), NT)
        s = jnp.where(piece_mask(limit_ref, SHIFTS[j % 4], j // 4), s, MASKED)
        s_ref[:, rows] = s
        for t in range(KEY_CHUNK // 128):
            peak = jnp.maximum(peak, s[:, 128 * t : 128 * t + 128])
    peak = jnp.max(peak, axis=1, keepdims=True) * factor
    own_p = jnp.exp2(own_s * factor - peak)
    total = own_p
    weighted = dot(own_p.astype(BF16), own_v, NN)
    for j in range(8):
        rows = slice(KEY_CHUNK * j, KEY_CHUNK * (j + 1))
        p = jnp.exp2(s_ref[:, rows] * factor - peak)
        for t in range(KEY_CHUNK // 128):
            total = total + p[:, 128 * t : 128 * t + 128]
        p16 = p.astype(BF16)
        p_ref[:, rows] = p16
        weighted = weighted + dot(p16, v_refs[j][...].reshape(KEY_CHUNK, 128), NN)
    total = jnp.sum(total, axis=1, keepdims=True)
    context = (weighted / total).astype(BF16)
    delta = jnp.sum(cg4.astype(F32) * context.astype(F32), axis=1, keepdims=True)
    attention = own_p / total
    own_ds = (attention * (dot(cg4, own_v, NT) - delta)).astype(BF16)
    grad = jnp.zeros((512, 128), F32)
    for j in range(8):
        rows = slice(KEY_CHUNK * j, KEY_CHUNK * (j + 1))
        dp = dot(cg4, v_refs[j][...].reshape(KEY_CHUNK, 128), NT)
        ds = (p_ref[:, rows].astype(F32) * (dp - delta)).astype(BF16)
        grad = grad + dot(ds, k_refs[j][...].reshape(KEY_CHUNK, 128), NN)
    grad = (grad / total + dot(own_ds, own_k, NN)) * INVERSE_ROOT
    grad = grad.astype(BF16)
    for g in range(4):
        ctx_ref[:, 128 * g : 128 * g + 128] = context[128 * g : 128 * g + 128]
        dq_ref[:, 128 * g : 128 * g + 128] = grad[128 * g : 128 * g + 128]
    dk_ref[...] = (dot(own_ds, q4, TN) * INVERSE_ROOT).astype(BF16)
    dv_ref[...] = dot(attention.astype(BF16), cg4, TN).astype(BF16)


def attention_call(part, limits, q, cg, own, pieces):
    first = 4 * part
    heads_in = pl.BlockSpec((BLOCK, 512), lambda k: (0, k + first))
    heads = pl.BlockSpec((BLOCK, 512), lambda k: (0, k))
    head = pl.BlockSpec((BLOCK, 128), lambda k: (0, k))
    return pl.pallas_call(
        attention_kernel,
        grid=(4,),
        out_shape=(
            jax.ShapeDtypeStruct((BLOCK, 2048), BF16),
            jax.ShapeDtypeStruct((BLOCK, 2048), BF16),
            jax.ShapeDtypeStruct((BLOCK, 512), BF16),
            jax.ShapeDtypeStruct((BLOCK, 512), BF16),
        ),
        in_specs=[
            smem(),
            heads_in,
            heads_in,
            pl.BlockSpec((BLOCK, 128), lambda k: (0, k + first)),
            pl.BlockSpec((BLOCK, 128), lambda k: (0, k + first + KV_HEADS)),
        ]
        + [pl.BlockSpec((4, 64, 128), lambda k: (0, 0, k))] * 8
        + [pl.BlockSpec((4, 64, 128), lambda k: (0, 0, k + 4))] * 8,
        out_specs=(heads, heads, head, head),
        scratch_shapes=[
            pltpu.VMEM((512, 2048), F32),
            pltpu.VMEM((512, 2048), BF16),
        ],
        compiler_params=pltpu.CompilerParams(
            dimension_semantics=("arbitrary",), vmem_limit_bytes=24 << 20
        ),
        cost_estimate=pl.CostEstimate(
            flops=12_000_000_000, bytes_accessed=8_000_000, transcendentals=4_000_000
        ),
    )(limits, q, cg, own, own, *pieces, *pieces)


def grads_kernel(
    mine_ref, x_ref, oc_ref, low_ref, upout_ref, pair_ref,
    *refs,
):
    out_ref = refs[8]
    low = low_ref[...]
    context, dq, dk, dv = (
        jnp.concatenate([refs[i][...], refs[i + 4][...]], axis=1) for i in range(4)
    )
    out_low = dot(wide_rows(mine_ref, 48, 64), context, NT).astype(BF16)
    up_q = (ADAPTER_SCALE * dot(wide_rows(mine_ref, 64, 80), dq, NT)).astype(BF16)
    up_k = (ADAPTER_SCALE * dot(pair_ref[:16], dk, NT)).astype(BF16)
    up_v = (ADAPTER_SCALE * dot(pair_ref[16:], dv, NT)).astype(BF16)
    up_low = jnp.concatenate([up_q, up_k, up_v], axis=0)
    up_out = upout_ref[...]
    for s in range(WIDE):
        cols = slice(128 * s, 128 * s + 128)
        out_ref[s, 0:48, :] = dot(up_low, x_ref[0, :, cols], NN).astype(BF16)
        out_ref[s, 48:64, :] = dot(up_out, context[:, cols], NN).astype(BF16)
        out_ref[s, 64:80, :] = (ADAPTER_SCALE * dot(low[:16], dq[:, cols], NN)).astype(BF16)
        out_ref[s, 80:96, :] = (ADAPTER_SCALE * dot(out_low, oc_ref[0, :, cols], NN)).astype(BF16)
    pairs = [
        ADAPTER_SCALE * dot(low[16:32], dk, NN),
        ADAPTER_SCALE * dot(low[32:48], dv, NN),
    ]
    for s in range(WIDE):
        cols = slice(32 * s, 32 * s + 32)
        out_ref[s, 96:104, :] = jnp.concatenate(
            [pairs[0][:8, cols], pairs[0][8:, cols], pairs[1][:8, cols], pairs[1][8:, cols]], axis=1
        ).astype(BF16)


def grads(mine, x, oc, low, up_out, pairs, *halves):
    return pl.pallas_call(
        grads_kernel,
        out_shape=jax.ShapeDtypeStruct((WIDE, ROWS, 128), BF16),
        in_specs=vmem(14),
        out_specs=pl.BlockSpec(memory_space=pltpu.VMEM),
        compiler_params=pltpu.CompilerParams(vmem_limit_bytes=28 << 20),
        name="grads",
    )(mine, x, oc, low, up_out, pairs, *halves)


def combine_kernel(ids_ref, lane_ref, back_ref, mine_ref, o1_ref, o2_ref, o3_ref, acc_ref):
    acc_ref[...] = jnp.zeros_like(acc_ref)

    def step(n, carry):
        a = ids_ref[0, n]
        acc_ref[a] += back_ref[n].astype(F32)
        return carry

    lax.fori_loop(0, WIDE, step, 0)
    y = lane_ref[0]
    mine_ref[...] = acc_ref[pl.ds(4 * y, 4)]
    for shift, ref in ((1, o1_ref), (2, o2_ref), (3, o3_ref)):
        ref[...] = acc_ref[pl.ds(4 * lax.rem(y + shift, 4), 4)].astype(BF16)


def combine(ids, place, back):
    quarter = (4, ROWS, 128)
    return pl.pallas_call(
        combine_kernel,
        out_shape=(
            jax.ShapeDtypeStruct(quarter, F32),
            jax.ShapeDtypeStruct(quarter, BF16),
            jax.ShapeDtypeStruct(quarter, BF16),
            jax.ShapeDtypeStruct(quarter, BF16),
        ),
        in_specs=[smem(), smem()] + vmem(1),
        out_specs=tuple(vmem(4)),
        scratch_shapes=[pltpu.VMEM((ADAPTERS, ROWS, 128), F32)],
        compiler_params=pltpu.CompilerParams(vmem_limit_bytes=8 << 20),
        name="combine",
    )(ids, place, back)


def quarter_kernel(mine_ref, r1_ref, r2_ref, r3_ref, out_ref):
    value = mine_ref[...]
    for ref in (r1_ref, r2_ref, r3_ref):
        value = value + ref[...].astype(F32)
    out_ref[...] = value.astype(BF16)


def add_kernel(a_ref, b_ref, out_ref):
    out_ref[...] = (a_ref[...].astype(F32) + b_ref[...].astype(F32)).astype(BF16)


def summed(kernel, *terms):
    return pl.pallas_call(
        kernel,
        out_shape=jax.ShapeDtypeStruct(terms[0].shape, BF16),
        in_specs=vmem(len(terms)),
        out_specs=pl.BlockSpec(memory_space=pltpu.VMEM),
        compiler_params=pltpu.CompilerParams(vmem_limit_bytes=4 << 20),
    )(*terms)


def unpack_kernel(lane_ref, q0_ref, q1_ref, q2_ref, q3_ref, down_ref, up_ref, pair_ref):
    y = lane_ref[0]
    for shift, ref in ((0, q0_ref), (1, q1_ref), (2, q2_ref), (3, q3_ref)):
        first = 4 * lax.rem(y + 4 - shift, 4)
        for t in range(4):
            a = first + t
            value = ref[t].astype(F32)
            for p in range(4):
                down_ref[a, p] = value[16 * p : 16 * p + 16]
            for p in range(2):
                up_ref[a, p] = value[64 + 16 * p : 80 + 16 * p]
                for h in range(2):
                    g = 2 * p + h
                    pair_ref[a, p, 8 * h : 8 * h + 8, :] = value[96:104, 32 * g : 32 * g + 32]


def unpack(place, quarters):
    return pl.pallas_call(
        unpack_kernel,
        out_shape=(
            jax.ShapeDtypeStruct((ADAPTERS, 4, RANK, 128), F32),
            jax.ShapeDtypeStruct((ADAPTERS, 2, RANK, 128), F32),
            jax.ShapeDtypeStruct((ADAPTERS, 2, RANK, 32), F32),
        ),
        in_specs=[smem()] + vmem(4),
        out_specs=tuple(vmem(3)),
        compiler_params=pltpu.CompilerParams(vmem_limit_bytes=8 << 20),
        name="unpack",
    )(place, *quarters)


def y_shift(value, shift):
    pairs = [(2 * y + z, 2 * ((y + shift) % 4) + z) for y in range(4) for z in range(2)]
    return lax.ppermute(value, "prompt", pairs)


def z_swap(value):
    return lax.ppermute(value, "prompt", [(p, p ^ 1) for p in range(8)])


def wide_index(x, z, core):
    return (4 * (x % 4) + z % 4) * 2 + core


def wide_move(value, dx, dz, dcore):
    pairs = [
        (wide_index(x, z, c), wide_index(x + dx, z + dz, c ^ dcore))
        for x in range(4) for z in range(4) for c in range(2)
    ]
    return lax.ppermute(value, "wide", pairs)


def gather_part(prompt, part):
    keys = prompt[:, 512 * part : 512 * part + 512]
    values = prompt[:, 1024 + 512 * part : 1536 + 512 * part]
    mine = jnp.concatenate([keys, values], axis=1)
    moved = [wide_move(mine, 0, s, 0) for s in (1, 2, 3)]
    column = jnp.stack([mine] + moved)
    return [column] + [wide_move(column, s, 0, 0) for s in (1, 3, 2)]


def step(
    candidate_hidden, frozen_query, candidate_key_value, prompt_key_value, candidate_adapter,
    prompt_block_end, adapter_down, adapter_up, adapter_up_key_value, output_cotangent,
    context_cotangent,
):
    group = lax.axis_index("prompt")
    place = jnp.stack([group // 2, group % 2]).astype(jnp.int32)
    lane = lax.axis_index("wide")
    limits = jnp.stack([lane // 8, lane // 2 % 4, lane % 2, prompt_block_end[0, 0]]).astype(jnp.int32)
    sent = pack(candidate_adapter, adapter_down, adapter_up, adapter_up_key_value)
    mine = lax.all_to_all(sent, "wide", 0, 0, tiled=True)
    parts = []
    for part in range(2):
        pieces = gather_part(prompt_key_value[0], part)
        parts.append(pieces + [wide_move(piece, 0, 0, 1) for piece in pieces])
    q, own, cg, low, up_out, pairs = prep(
        mine, candidate_hidden, frozen_query, candidate_key_value, output_cotangent,
        context_cotangent,
    )
    halves = []
    for part in range(2):
        halves += attention_call(part, limits, q, cg, own, parts[part])
    blocks = grads(mine, candidate_hidden, output_cotangent, low, up_out, pairs, *halves)
    back = lax.all_to_all(blocks, "wide", 0, 0, tiled=True)
    total, *others = combine(candidate_adapter, place, back)
    received = [y_shift(other, shift) for shift, other in zip((1, 2, 3), others)]
    quarter = summed(quarter_kernel, total, *received)
    quarter = summed(add_kernel, quarter, z_swap(quarter))
    quarters = [quarter] + [y_shift(quarter, shift) for shift in (1, 2, 3)]
    return unpack(place, quarters)


def solution(mesh):
    tokens = P("prompt", "wide", None)
    columns = P(None, None, None, "wide")
    placed = (
        tokens, tokens, tokens, tokens, P("prompt", None), P("prompt", "wide"),
        columns, columns, columns, tokens, tokens,
    )
    return jax.shard_map(
        step, mesh=mesh, in_specs=placed, out_specs=(columns, columns, columns), check_vma=False
    )
```

```python
import jax
import jax.numpy as jnp
from jax import lax
from jax.experimental import pallas as pl
from jax.experimental.pallas import tpu as pltpu
from jax.sharding import PartitionSpec as P


KV_HEADS = 8
HEAD_DIM = 128
ADAPTERS = 16
RANK = 16
BLOCK = 128
WIDE = 32
ROWS = 104
ADAPTER_SCALE = 2.0
MASKED = -1e30
INVERSE_ROOT = HEAD_DIM ** (-0.5)
LOG2E = 1.4426950408889634
KEY_CHUNK = 256
SHIFTS = (0, 1, 3, 2)
HALVES = (slice(0, 256), slice(256, 512))

BF16 = jnp.bfloat16
F32 = jnp.float32


def dot(a, b, dims):
    return lax.dot_general(a, b, (dims, ((), ())), preferred_element_type=F32)


NN = ((1,), (0,))
NT = ((1,), (1,))
TN = ((0,), (0,))


def vmem(n):
    return [pl.BlockSpec(memory_space=pltpu.VMEM)] * n


def smem():
    return pl.BlockSpec(memory_space=pltpu.SMEM)


def pack_kernel(ids_ref, end_ref, down_ref, up_ref, pair_ref, out_ref, place_ref):
    lane = lax.axis_index("wide")
    group = lax.axis_index("prompt")
    numbers = (lane // 8, lax.rem(lane // 2, 4), lax.rem(lane, 2), end_ref[0, 0])
    for i, value in enumerate(numbers + (group // 2, lax.rem(group, 2))):
        place_ref[i] = value

    def step(n, carry):
        a = ids_ref[0, n]
        for p in range(4):
            out_ref[n, 16 * p : 16 * p + 16, :] = down_ref[a, p]
        for p in range(2):
            out_ref[n, 64 + 16 * p : 80 + 16 * p, :] = up_ref[a, p]
        pieces = []
        for p in range(2):
            pair = pair_ref[a, p].astype(F32)
            pieces += [pair[:8], pair[8:]]
        out_ref[n, 96:104, :] = jnp.concatenate(pieces, axis=1).astype(BF16)
        return carry

    lax.fori_loop(0, WIDE, step, 0)


def pack(ids, end, down, up, pairs):
    return pl.pallas_call(
        pack_kernel,
        out_shape=(
            jax.ShapeDtypeStruct((WIDE, ROWS, 128), BF16),
            jax.ShapeDtypeStruct((8,), jnp.int32),
        ),
        in_specs=[smem(), smem()] + vmem(3),
        out_specs=(pl.BlockSpec(memory_space=pltpu.VMEM), smem()),
        compiler_params=pltpu.CompilerParams(vmem_limit_bytes=4 << 20),
        name="pack",
    )(ids, end, down, up, pairs)


def split_kernel(prompt_ref, first_ref, second_ref):
    for part, ref in enumerate((first_ref, second_ref)):
        ref[:, :512] = prompt_ref[0, :, 512 * part : 512 * part + 512]
        ref[:, 512:] = prompt_ref[0, :, 1024 + 512 * part : 1536 + 512 * part]


def split_prompt(prompt):
    half = jax.ShapeDtypeStruct((64, 1024), BF16)
    return pl.pallas_call(
        split_kernel,
        out_shape=(half, half),
        in_specs=vmem(1),
        out_specs=tuple(vmem(2)),
        compiler_params=pltpu.CompilerParams(vmem_limit_bytes=2 << 20),
        name="split",
    )(prompt)


def column_kernel(a_ref, b_ref, c_ref, d_ref, out_ref):
    for i, ref in enumerate((a_ref, b_ref, c_ref, d_ref)):
        out_ref[i] = ref[...]


def column_of(pieces):
    return pl.pallas_call(
        column_kernel,
        out_shape=jax.ShapeDtypeStruct((4, 64, 1024), BF16),
        in_specs=vmem(4),
        out_specs=pl.BlockSpec(memory_space=pltpu.VMEM),
        compiler_params=pltpu.CompilerParams(vmem_limit_bytes=4 << 20),
        name="column",
    )(*pieces)


def wide_rows(ref, start, stop):
    return jnp.concatenate([ref[s, start:stop, :] for s in range(WIDE)], axis=1)


def pair_rows(ref):
    parts = []
    for g in range(4):
        pieces = []
        for s in range(WIDE):
            pieces.append(ref[s, 96:104, 32 * g : 32 * g + 32].astype(F32))
        parts.append(jnp.concatenate(pieces, axis=1))
    return jnp.concatenate(parts, axis=0).astype(BF16)


def prep_kernel(
    mine_ref, x_ref, fq_ref, ckv_ref, oc_ref, cc_ref,
    q_ref, own_ref, cg_ref, low_ref, upout_ref, pair_ref,
):
    low = dot(wide_rows(mine_ref, 0, 48), x_ref[0], NT).astype(BF16)
    low_ref[...] = low
    up_out = (ADAPTER_SCALE * dot(wide_rows(mine_ref, 80, 96), oc_ref[0], NT)).astype(BF16)
    upout_ref[...] = up_out
    pairs = pair_rows(mine_ref)
    pair_ref[...] = pairs
    for s in range(WIDE):
        cols = slice(128 * s, 128 * s + 128)
        delta = dot(low[:16], mine_ref[s, 64:80, :], TN)
        q_ref[:, cols] = (fq_ref[0, :, cols].astype(F32) + ADAPTER_SCALE * delta).astype(BF16)
        delta = dot(up_out, mine_ref[s, 48:64, :], TN)
        cg_ref[:, cols] = (cc_ref[0, :, cols].astype(F32) + delta).astype(BF16)
    for h in range(2):
        cols = slice(1024 * h, 1024 * h + 1024)
        delta = dot(low[16 + 16 * h : 32 + 16 * h], pairs[16 * h : 16 * h + 16], TN)
        own_ref[:, cols] = (ckv_ref[0, :, cols].astype(F32) + ADAPTER_SCALE * delta).astype(BF16)


def prep(mine, x, fq, ckv, oc, cc):
    return pl.pallas_call(
        prep_kernel,
        out_shape=(
            jax.ShapeDtypeStruct((BLOCK, 4096), BF16),
            jax.ShapeDtypeStruct((BLOCK, 2048), BF16),
            jax.ShapeDtypeStruct((BLOCK, 4096), BF16),
            jax.ShapeDtypeStruct((48, 128), BF16),
            jax.ShapeDtypeStruct((16, 128), BF16),
            jax.ShapeDtypeStruct((32, 1024), BF16),
        ),
        in_specs=vmem(6),
        out_specs=tuple(vmem(6)),
        compiler_params=pltpu.CompilerParams(vmem_limit_bytes=12 << 20),
        name="prep",
    )(mine, x, fq, ckv, oc, cc)


def stack_heads(ref):
    return jnp.concatenate([ref[:, 128 * g : 128 * g + 128] for g in range(4)], axis=0)


def piece_mask(limit_ref, shift, other):
    x, z, core, end = (limit_ref[i] for i in range(4))
    side = core ^ other
    lane = lax.broadcasted_iota(jnp.int32, (1, KEY_CHUNK), 1)
    origin = jnp.zeros((1, KEY_CHUNK), jnp.int32)
    for t in range(4):
        source = (lax.rem(x + 4 - shift, 4) * 4 + lax.rem(z + 4 - t, 4)) * 2 + side
        origin = jnp.where(lane >= 64 * t, source, origin)
    return origin < 2 * end


def attention_kernel(
    limit_ref, q_ref, cg_ref, ok_ref, ov_ref, *refs,
):
    k_refs, v_refs = refs[:8], refs[8:16]
    ctx_ref, dq_ref, dk_ref, dv_ref, s_ref, p_ref = refs[16:]
    factor = INVERSE_ROOT * LOG2E
    q4 = stack_heads(q_ref)
    cg4 = stack_heads(cg_ref)
    own_k = ok_ref[...]
    own_v = ov_ref[...]
    row = lax.broadcasted_iota(jnp.int32, (512, BLOCK), 0) & (BLOCK - 1)
    col = lax.broadcasted_iota(jnp.int32, (512, BLOCK), 1)
    own_s = jnp.where(col <= row, dot(q4, own_k, NT), MASKED)
    peak = own_s
    for j in range(8):
        rows = slice(KEY_CHUNK * j, KEY_CHUNK * (j + 1))
        s = dot(q4, k_refs[j][...].reshape(KEY_CHUNK, 128), NT)
        s = jnp.where(piece_mask(limit_ref, SHIFTS[j % 4], j // 4), s, MASKED)
        s_ref[:, rows] = s
        for t in range(KEY_CHUNK // 128):
            peak = jnp.maximum(peak, s[:, 128 * t : 128 * t + 128])
    peak = jnp.max(peak, axis=1, keepdims=True) * factor
    own_p = jnp.exp2(own_s * factor - peak)
    total = own_p
    own_p16 = own_p.astype(BF16)
    weighted = [dot(own_p16[r], own_v, NN) for r in HALVES]
    for j in range(8):
        rows = slice(KEY_CHUNK * j, KEY_CHUNK * (j + 1))
        p = jnp.exp2(s_ref[:, rows] * factor - peak)
        for t in range(KEY_CHUNK // 128):
            total = total + p[:, 128 * t : 128 * t + 128]
        p16 = p.astype(BF16)
        p_ref[:, rows] = p16
        value = v_refs[j][...].reshape(KEY_CHUNK, 128)
        weighted = [w + dot(p16[r], value, NN) for w, r in zip(weighted, HALVES)]
    total = jnp.sum(total, axis=1, keepdims=True)
    context = (jnp.concatenate(weighted, axis=0) / total).astype(BF16)
    delta = jnp.sum(cg4.astype(F32) * context.astype(F32), axis=1, keepdims=True)
    attention = own_p / total
    own_ds = (attention * (dot(cg4, own_v, NT) - delta)).astype(BF16)
    grad = [jnp.zeros((256, 128), F32)] * 2
    for j in range(8):
        rows = slice(KEY_CHUNK * j, KEY_CHUNK * (j + 1))
        dp = dot(cg4, v_refs[j][...].reshape(KEY_CHUNK, 128), NT)
        ds = (p_ref[:, rows].astype(F32) * (dp - delta)).astype(BF16)
        key = k_refs[j][...].reshape(KEY_CHUNK, 128)
        grad = [w + dot(ds[r], key, NN) for w, r in zip(grad, HALVES)]
    grad = (jnp.concatenate(grad, axis=0) / total + dot(own_ds, own_k, NN)) * INVERSE_ROOT
    grad = grad.astype(BF16)
    for g in range(4):
        ctx_ref[:, 128 * g : 128 * g + 128] = context[128 * g : 128 * g + 128]
        dq_ref[:, 128 * g : 128 * g + 128] = grad[128 * g : 128 * g + 128]
    dk_ref[...] = (dot(own_ds, q4, TN) * INVERSE_ROOT).astype(BF16)
    dv_ref[...] = dot(attention.astype(BF16), cg4, TN).astype(BF16)


def attention_call(part, place, q, cg, own, pieces):
    first = 4 * part
    heads_in = pl.BlockSpec((BLOCK, 512), lambda k: (0, k + first))
    heads = pl.BlockSpec((BLOCK, 512), lambda k: (0, k))
    head = pl.BlockSpec((BLOCK, 128), lambda k: (0, k))
    return pl.pallas_call(
        attention_kernel,
        grid=(4,),
        out_shape=(
            jax.ShapeDtypeStruct((BLOCK, 2048), BF16),
            jax.ShapeDtypeStruct((BLOCK, 2048), BF16),
            jax.ShapeDtypeStruct((BLOCK, 512), BF16),
            jax.ShapeDtypeStruct((BLOCK, 512), BF16),
        ),
        in_specs=[
            smem(),
            heads_in,
            heads_in,
            pl.BlockSpec((BLOCK, 128), lambda k: (0, k + first)),
            pl.BlockSpec((BLOCK, 128), lambda k: (0, k + first + KV_HEADS)),
        ]
        + [pl.BlockSpec((4, 64, 128), lambda k: (0, 0, k))] * 8
        + [pl.BlockSpec((4, 64, 128), lambda k: (0, 0, k + 4))] * 8,
        out_specs=(heads, heads, head, head),
        scratch_shapes=[
            pltpu.VMEM((512, 2048), F32),
            pltpu.VMEM((512, 2048), BF16),
        ],
        compiler_params=pltpu.CompilerParams(
            dimension_semantics=("arbitrary",), vmem_limit_bytes=18 << 20
        ),
        cost_estimate=pl.CostEstimate(
            flops=12_000_000_000, bytes_accessed=8_000_000, transcendentals=4_000_000
        ),
    )(place, q, cg, own, own, *pieces, *pieces)


def grads_kernel(
    mine_ref, x_ref, oc_ref, low_ref, upout_ref, pair_ref,
    *refs,
):
    out_ref = refs[8]
    low = low_ref[...]
    context, dq, dk, dv = (
        jnp.concatenate([refs[i][...], refs[i + 4][...]], axis=1) for i in range(4)
    )
    out_low = dot(wide_rows(mine_ref, 48, 64), context, NT).astype(BF16)
    up_q = (ADAPTER_SCALE * dot(wide_rows(mine_ref, 64, 80), dq, NT)).astype(BF16)
    up_k = (ADAPTER_SCALE * dot(pair_ref[:16], dk, NT)).astype(BF16)
    up_v = (ADAPTER_SCALE * dot(pair_ref[16:], dv, NT)).astype(BF16)
    up_low = jnp.concatenate([up_q, up_k, up_v], axis=0)
    up_out = upout_ref[...]
    for s in range(WIDE):
        cols = slice(128 * s, 128 * s + 128)
        out_ref[s, 0:48, :] = dot(up_low, x_ref[0, :, cols], NN).astype(BF16)
        out_ref[s, 48:64, :] = dot(up_out, context[:, cols], NN).astype(BF16)
        out_ref[s, 64:80, :] = (ADAPTER_SCALE * dot(low[:16], dq[:, cols], NN)).astype(BF16)
        out_ref[s, 80:96, :] = (ADAPTER_SCALE * dot(out_low, oc_ref[0, :, cols], NN)).astype(BF16)
    pairs = [
        ADAPTER_SCALE * dot(low[16:32], dk, NN),
        ADAPTER_SCALE * dot(low[32:48], dv, NN),
    ]
    for s in range(WIDE):
        cols = slice(32 * s, 32 * s + 32)
        out_ref[s, 96:104, :] = jnp.concatenate(
            [pairs[0][:8, cols], pairs[0][8:, cols], pairs[1][:8, cols], pairs[1][8:, cols]], axis=1
        ).astype(BF16)


def grads(mine, x, oc, low, up_out, pairs, *halves):
    return pl.pallas_call(
        grads_kernel,
        out_shape=jax.ShapeDtypeStruct((WIDE, ROWS, 128), BF16),
        in_specs=vmem(14),
        out_specs=pl.BlockSpec(memory_space=pltpu.VMEM),
        compiler_params=pltpu.CompilerParams(vmem_limit_bytes=12 << 20),
        name="grads",
    )(mine, x, oc, low, up_out, pairs, *halves)


def combine_kernel(ids_ref, lane_ref, back_ref, mine_ref, o1_ref, o2_ref, o3_ref, acc_ref):
    acc_ref[...] = jnp.zeros_like(acc_ref)

    def step(n, carry):
        a = ids_ref[0, n]
        acc_ref[a] += back_ref[n].astype(F32)
        return carry

    lax.fori_loop(0, WIDE, step, 0)
    y = lane_ref[4]
    mine_ref[...] = acc_ref[pl.ds(4 * y, 4)]
    for shift, ref in ((1, o1_ref), (2, o2_ref), (3, o3_ref)):
        ref[...] = acc_ref[pl.ds(4 * lax.rem(y + shift, 4), 4)].astype(BF16)


def combine(ids, place, back):
    quarter = (4, ROWS, 128)
    return pl.pallas_call(
        combine_kernel,
        out_shape=(
            jax.ShapeDtypeStruct(quarter, F32),
            jax.ShapeDtypeStruct(quarter, BF16),
            jax.ShapeDtypeStruct(quarter, BF16),
            jax.ShapeDtypeStruct(quarter, BF16),
        ),
        in_specs=[smem(), smem()] + vmem(1),
        out_specs=tuple(vmem(4)),
        scratch_shapes=[pltpu.VMEM((ADAPTERS, ROWS, 128), F32)],
        compiler_params=pltpu.CompilerParams(vmem_limit_bytes=8 << 20),
        name="combine",
    )(ids, place, back)


def quarter_kernel(mine_ref, r1_ref, r2_ref, r3_ref, out_ref):
    value = mine_ref[...]
    for ref in (r1_ref, r2_ref, r3_ref):
        value = value + ref[...].astype(F32)
    out_ref[...] = value.astype(BF16)


def add_kernel(a_ref, b_ref, out_ref):
    out_ref[...] = (a_ref[...].astype(F32) + b_ref[...].astype(F32)).astype(BF16)


def summed(kernel, *terms):
    return pl.pallas_call(
        kernel,
        out_shape=jax.ShapeDtypeStruct(terms[0].shape, BF16),
        in_specs=vmem(len(terms)),
        out_specs=pl.BlockSpec(memory_space=pltpu.VMEM),
        compiler_params=pltpu.CompilerParams(vmem_limit_bytes=4 << 20),
    )(*terms)


def unpack_kernel(lane_ref, q0_ref, q1_ref, q2_ref, q3_ref, down_ref, up_ref, pair_ref):
    y = lane_ref[4]
    for shift, ref in ((0, q0_ref), (1, q1_ref), (2, q2_ref), (3, q3_ref)):
        first = 4 * lax.rem(y + 4 - shift, 4)
        for t in range(4):
            a = first + t
            value = ref[t].astype(F32)
            for p in range(4):
                down_ref[a, p] = value[16 * p : 16 * p + 16]
            for p in range(2):
                up_ref[a, p] = value[64 + 16 * p : 80 + 16 * p]
                for h in range(2):
                    g = 2 * p + h
                    pair_ref[a, p, 8 * h : 8 * h + 8, :] = value[96:104, 32 * g : 32 * g + 32]


def unpack(place, quarters):
    return pl.pallas_call(
        unpack_kernel,
        out_shape=(
            jax.ShapeDtypeStruct((ADAPTERS, 4, RANK, 128), F32),
            jax.ShapeDtypeStruct((ADAPTERS, 2, RANK, 128), F32),
            jax.ShapeDtypeStruct((ADAPTERS, 2, RANK, 32), F32),
        ),
        in_specs=[smem()] + vmem(4),
        out_specs=tuple(vmem(3)),
        compiler_params=pltpu.CompilerParams(vmem_limit_bytes=8 << 20),
        name="unpack",
    )(place, *quarters)


def y_shift(value, shift):
    pairs = [(2 * y + z, 2 * ((y + shift) % 4) + z) for y in range(4) for z in range(2)]
    return lax.ppermute(value, "prompt", pairs)


def z_swap(value):
    return lax.ppermute(value, "prompt", [(p, p ^ 1) for p in range(8)])


def wide_index(x, z, core):
    return (4 * (x % 4) + z % 4) * 2 + core


def wide_move(value, dx, dz, dcore):
    pairs = [
        (wide_index(x, z, c), wide_index(x + dx, z + dz, c ^ dcore))
        for x in range(4) for z in range(4) for c in range(2)
    ]
    return lax.ppermute(value, "wide", pairs)


def gather_part(mine):
    moved = [wide_move(mine, 0, s, 0) for s in (1, 2, 3)]
    column = column_of([mine] + moved)
    return [column] + [wide_move(column, s, 0, 0) for s in (1, 3, 2)]


def step(
    candidate_hidden, frozen_query, candidate_key_value, prompt_key_value, candidate_adapter,
    prompt_block_end, adapter_down, adapter_up, adapter_up_key_value, output_cotangent,
    context_cotangent,
):
    prompts = split_prompt(prompt_key_value)
    sent, place = pack(
        candidate_adapter, prompt_block_end, adapter_down, adapter_up, adapter_up_key_value
    )
    mine = lax.all_to_all(sent, "wide", 0, 0, tiled=True)
    parts = []
    for part in range(2):
        pieces = gather_part(prompts[part])
        parts.append(pieces + [wide_move(piece, 0, 0, 1) for piece in pieces])
    q, own, cg, low, up_out, pairs = prep(
        mine, candidate_hidden, frozen_query, candidate_key_value, output_cotangent,
        context_cotangent,
    )
    halves = []
    for part in range(2):
        halves += attention_call(part, place, q, cg, own, parts[part])
    blocks = grads(mine, candidate_hidden, output_cotangent, low, up_out, pairs, *halves)
    back = lax.all_to_all(blocks, "wide", 0, 0, tiled=True)
    total, *others = combine(candidate_adapter, place, back)
    received = [y_shift(other, shift) for shift, other in zip((1, 2, 3), others)]
    quarter = summed(quarter_kernel, total, *received)
    quarter = summed(add_kernel, quarter, z_swap(quarter))
    quarters = [quarter] + [y_shift(quarter, shift) for shift in (1, 2, 3)]
    return unpack(place, quarters)


def solution(mesh):
    tokens = P("prompt", "wide", None)
    columns = P(None, None, None, "wide")
    placed = (
        tokens, tokens, tokens, tokens, P("prompt", None), P("prompt", "wide"),
        columns, columns, columns, tokens, tokens,
    )
    return jax.shard_map(
        step, mesh=mesh, in_specs=placed, out_specs=(columns, columns, columns), check_vma=False
    )
```

```python
import jax
import jax.numpy as jnp
from jax import lax
from jax.experimental import pallas as pl
from jax.experimental.pallas import tpu as pltpu
from jax.sharding import PartitionSpec as P


KV_HEADS = 8
HEAD_DIM = 128
ADAPTERS = 16
RANK = 16
BLOCK = 128
WIDE = 32
ROWS = 104
ADAPTER_SCALE = 2.0
MASKED = -1e30
INVERSE_ROOT = HEAD_DIM ** (-0.5)
LOG2E = 1.4426950408889634
KEY_CHUNK = 256
SHIFTS = (0, 1, 3, 2)
HALVES = (slice(0, 256), slice(256, 512))

BF16 = jnp.bfloat16
F32 = jnp.float32


def dot(a, b, dims):
    return lax.dot_general(a, b, (dims, ((), ())), preferred_element_type=F32)


NN = ((1,), (0,))
NT = ((1,), (1,))
TN = ((0,), (0,))


def vmem(n):
    return [pl.BlockSpec(memory_space=pltpu.VMEM)] * n


def smem():
    return pl.BlockSpec(memory_space=pltpu.SMEM)


def pack_kernel(ids_ref, end_ref, down_ref, up_ref, pair_ref, out_ref, place_ref, joined_ref):
    lane = lax.axis_index("wide")
    group = lax.axis_index("prompt")
    numbers = (lane // 8, lax.rem(lane // 2, 4), lax.rem(lane, 2), end_ref[0, 0])
    for i, value in enumerate(numbers + (group // 2, lax.rem(group, 2))):
        place_ref[i] = value

    for a in range(ADAPTERS):
        pieces = []
        for p in range(2):
            pair = pair_ref[a, p].astype(F32)
            pieces += [pair[:8], pair[8:]]
        joined_ref[a] = jnp.concatenate(pieces, axis=1)
    for n in range(WIDE):
        a = ids_ref[0, n]
        for p in range(4):
            out_ref[n, 16 * p : 16 * p + 16, :] = down_ref[a, p]
        for p in range(2):
            out_ref[n, 64 + 16 * p : 80 + 16 * p, :] = up_ref[a, p]
        out_ref[n, 96:104, :] = joined_ref[a].astype(BF16)


def pack(ids, end, down, up, pairs):
    return pl.pallas_call(
        pack_kernel,
        out_shape=(
            jax.ShapeDtypeStruct((WIDE, ROWS, 128), BF16),
            jax.ShapeDtypeStruct((8,), jnp.int32),
        ),
        in_specs=[smem(), smem()] + vmem(3),
        out_specs=(pl.BlockSpec(memory_space=pltpu.VMEM), smem()),
        scratch_shapes=[pltpu.VMEM((ADAPTERS, 8, 128), F32)],
        compiler_params=pltpu.CompilerParams(vmem_limit_bytes=4 << 20),
        name="pack",
    )(ids, end, down, up, pairs)


def split_kernel(prompt_ref, first_ref, second_ref):
    for part, ref in enumerate((first_ref, second_ref)):
        ref[:, :512] = prompt_ref[0, :, 512 * part : 512 * part + 512]
        ref[:, 512:] = prompt_ref[0, :, 1024 + 512 * part : 1536 + 512 * part]


def split_prompt(prompt):
    half = jax.ShapeDtypeStruct((64, 1024), BF16)
    return pl.pallas_call(
        split_kernel,
        out_shape=(half, half),
        in_specs=vmem(1),
        out_specs=tuple(vmem(2)),
        compiler_params=pltpu.CompilerParams(vmem_limit_bytes=2 << 20),
        name="split",
    )(prompt)


def column_kernel(a_ref, b_ref, c_ref, d_ref, out_ref):
    for i, ref in enumerate((a_ref, b_ref, c_ref, d_ref)):
        out_ref[i] = ref[...]


def column_of(pieces):
    return pl.pallas_call(
        column_kernel,
        out_shape=jax.ShapeDtypeStruct((4, 64, 1024), BF16),
        in_specs=vmem(4),
        out_specs=pl.BlockSpec(memory_space=pltpu.VMEM),
        compiler_params=pltpu.CompilerParams(vmem_limit_bytes=4 << 20),
        name="column",
    )(*pieces)


def wide_rows(ref, start, stop):
    return jnp.concatenate([ref[s, start:stop, :] for s in range(WIDE)], axis=1)


def pair_rows(ref):
    parts = []
    for g in range(4):
        pieces = []
        for s in range(WIDE):
            pieces.append(ref[s, 96:104, 32 * g : 32 * g + 32].astype(F32))
        parts.append(jnp.concatenate(pieces, axis=1))
    return jnp.concatenate(parts, axis=0).astype(BF16)


def prep_kernel(
    mine_ref, x_ref, fq_ref, ckv_ref, oc_ref, cc_ref,
    q_ref, own_ref, cg_ref, low_ref, upout_ref, pair_ref,
):
    low = dot(wide_rows(mine_ref, 0, 48), x_ref[0], NT).astype(BF16)
    low_ref[...] = low
    up_out = (ADAPTER_SCALE * dot(wide_rows(mine_ref, 80, 96), oc_ref[0], NT)).astype(BF16)
    upout_ref[...] = up_out
    pairs = pair_rows(mine_ref)
    pair_ref[...] = pairs
    for s in range(WIDE):
        cols = slice(128 * s, 128 * s + 128)
        delta = dot(low[:16], mine_ref[s, 64:80, :], TN)
        q_ref[:, cols] = (fq_ref[0, :, cols].astype(F32) + ADAPTER_SCALE * delta).astype(BF16)
        delta = dot(up_out, mine_ref[s, 48:64, :], TN)
        cg_ref[:, cols] = (cc_ref[0, :, cols].astype(F32) + delta).astype(BF16)
    for h in range(2):
        cols = slice(1024 * h, 1024 * h + 1024)
        delta = dot(low[16 + 16 * h : 32 + 16 * h], pairs[16 * h : 16 * h + 16], TN)
        own_ref[:, cols] = (ckv_ref[0, :, cols].astype(F32) + ADAPTER_SCALE * delta).astype(BF16)


def prep(mine, x, fq, ckv, oc, cc):
    return pl.pallas_call(
        prep_kernel,
        out_shape=(
            jax.ShapeDtypeStruct((BLOCK, 4096), BF16),
            jax.ShapeDtypeStruct((BLOCK, 2048), BF16),
            jax.ShapeDtypeStruct((BLOCK, 4096), BF16),
            jax.ShapeDtypeStruct((48, 128), BF16),
            jax.ShapeDtypeStruct((16, 128), BF16),
            jax.ShapeDtypeStruct((32, 1024), BF16),
        ),
        in_specs=vmem(6),
        out_specs=tuple(vmem(6)),
        compiler_params=pltpu.CompilerParams(vmem_limit_bytes=12 << 20),
        name="prep",
    )(mine, x, fq, ckv, oc, cc)


def stack_heads(ref):
    return jnp.concatenate([ref[:, 128 * g : 128 * g + 128] for g in range(4)], axis=0)


def piece_mask(limit_ref, shift, other):
    x, z, core, end = (limit_ref[i] for i in range(4))
    side = core ^ other
    lane = lax.broadcasted_iota(jnp.int32, (1, KEY_CHUNK), 1)
    origin = jnp.zeros((1, KEY_CHUNK), jnp.int32)
    for t in range(4):
        source = (lax.rem(x + 4 - shift, 4) * 4 + lax.rem(z + 4 - t, 4)) * 2 + side
        origin = jnp.where(lane >= 64 * t, source, origin)
    return origin < 2 * end


def attention_kernel(
    limit_ref, q_ref, cg_ref, ok_ref, ov_ref, *refs,
):
    k_refs, v_refs = refs[:8], refs[8:16]
    ctx_ref, dq_ref, dk_ref, dv_ref, s_ref, p_ref = refs[16:]
    factor = INVERSE_ROOT * LOG2E
    q4 = stack_heads(q_ref)
    cg4 = stack_heads(cg_ref)
    own_k = ok_ref[...]
    own_v = ov_ref[...]
    row = lax.broadcasted_iota(jnp.int32, (512, BLOCK), 0) & (BLOCK - 1)
    col = lax.broadcasted_iota(jnp.int32, (512, BLOCK), 1)
    own_s = jnp.where(col <= row, dot(q4, own_k, NT), MASKED)
    peak = own_s
    for j in range(8):
        rows = slice(KEY_CHUNK * j, KEY_CHUNK * (j + 1))
        s = dot(q4, k_refs[j][...].reshape(KEY_CHUNK, 128), NT)
        s = jnp.where(piece_mask(limit_ref, SHIFTS[j % 4], j // 4), s, MASKED)
        s_ref[:, rows] = s
        for t in range(KEY_CHUNK // 128):
            peak = jnp.maximum(peak, s[:, 128 * t : 128 * t + 128])
    peak = jnp.max(peak, axis=1, keepdims=True) * factor
    own_p = jnp.exp2(own_s * factor - peak)
    total = own_p
    own_p16 = own_p.astype(BF16)
    weighted = [dot(own_p16[r], own_v, NN) for r in HALVES]
    for j in range(8):
        rows = slice(KEY_CHUNK * j, KEY_CHUNK * (j + 1))
        p = jnp.exp2(s_ref[:, rows] * factor - peak)
        for t in range(KEY_CHUNK // 128):
            total = total + p[:, 128 * t : 128 * t + 128]
        p16 = p.astype(BF16)
        p_ref[:, rows] = p16
        value = v_refs[j][...].reshape(KEY_CHUNK, 128)
        weighted = [w + dot(p16[r], value, NN) for w, r in zip(weighted, HALVES)]
    total = jnp.sum(total, axis=1, keepdims=True)
    context = (jnp.concatenate(weighted, axis=0) / total).astype(BF16)
    delta = jnp.sum(cg4.astype(F32) * context.astype(F32), axis=1, keepdims=True)
    attention = own_p / total
    own_ds = (attention * (dot(cg4, own_v, NT) - delta)).astype(BF16)
    grad = [jnp.zeros((256, 128), F32)] * 2
    for j in range(8):
        rows = slice(KEY_CHUNK * j, KEY_CHUNK * (j + 1))
        dp = dot(cg4, v_refs[j][...].reshape(KEY_CHUNK, 128), NT)
        ds = (p_ref[:, rows].astype(F32) * (dp - delta)).astype(BF16)
        key = k_refs[j][...].reshape(KEY_CHUNK, 128)
        grad = [w + dot(ds[r], key, NN) for w, r in zip(grad, HALVES)]
    grad = (jnp.concatenate(grad, axis=0) / total + dot(own_ds, own_k, NN)) * INVERSE_ROOT
    grad = grad.astype(BF16)
    for g in range(4):
        ctx_ref[:, 128 * g : 128 * g + 128] = context[128 * g : 128 * g + 128]
        dq_ref[:, 128 * g : 128 * g + 128] = grad[128 * g : 128 * g + 128]
    dk_ref[...] = (dot(own_ds, q4, TN) * INVERSE_ROOT).astype(BF16)
    dv_ref[...] = dot(attention.astype(BF16), cg4, TN).astype(BF16)


def attention_call(part, place, q, cg, own, pieces):
    first = 4 * part
    heads_in = pl.BlockSpec((BLOCK, 512), lambda k: (0, k + first))
    heads = pl.BlockSpec((BLOCK, 512), lambda k: (0, k))
    head = pl.BlockSpec((BLOCK, 128), lambda k: (0, k))
    return pl.pallas_call(
        attention_kernel,
        grid=(4,),
        out_shape=(
            jax.ShapeDtypeStruct((BLOCK, 2048), BF16),
            jax.ShapeDtypeStruct((BLOCK, 2048), BF16),
            jax.ShapeDtypeStruct((BLOCK, 512), BF16),
            jax.ShapeDtypeStruct((BLOCK, 512), BF16),
        ),
        in_specs=[
            smem(),
            heads_in,
            heads_in,
            pl.BlockSpec((BLOCK, 128), lambda k: (0, k + first)),
            pl.BlockSpec((BLOCK, 128), lambda k: (0, k + first + KV_HEADS)),
        ]
        + [pl.BlockSpec((4, 64, 128), lambda k: (0, 0, k))] * 8
        + [pl.BlockSpec((4, 64, 128), lambda k: (0, 0, k + 4))] * 8,
        out_specs=(heads, heads, head, head),
        scratch_shapes=[
            pltpu.VMEM((512, 2048), F32),
            pltpu.VMEM((512, 2048), BF16),
        ],
        compiler_params=pltpu.CompilerParams(
            dimension_semantics=("arbitrary",), vmem_limit_bytes=18 << 20
        ),
        cost_estimate=pl.CostEstimate(
            flops=12_000_000_000, bytes_accessed=8_000_000, transcendentals=4_000_000
        ),
    )(place, q, cg, own, own, *pieces, *pieces)


def grads_kernel(
    mine_ref, x_ref, oc_ref, low_ref, upout_ref, pair_ref,
    *refs,
):
    out_ref = refs[8]
    low = low_ref[...]
    context, dq, dk, dv = (
        jnp.concatenate([refs[i][...], refs[i + 4][...]], axis=1) for i in range(4)
    )
    out_low = dot(wide_rows(mine_ref, 48, 64), context, NT).astype(BF16)
    up_q = (ADAPTER_SCALE * dot(wide_rows(mine_ref, 64, 80), dq, NT)).astype(BF16)
    up_k = (ADAPTER_SCALE * dot(pair_ref[:16], dk, NT)).astype(BF16)
    up_v = (ADAPTER_SCALE * dot(pair_ref[16:], dv, NT)).astype(BF16)
    up_low = jnp.concatenate([up_q, up_k, up_v], axis=0)
    up_out = upout_ref[...]
    for s in range(WIDE):
        cols = slice(128 * s, 128 * s + 128)
        out_ref[s, 0:48, :] = dot(up_low, x_ref[0, :, cols], NN).astype(BF16)
        out_ref[s, 48:64, :] = dot(up_out, context[:, cols], NN).astype(BF16)
        out_ref[s, 64:80, :] = (ADAPTER_SCALE * dot(low[:16], dq[:, cols], NN)).astype(BF16)
        out_ref[s, 80:96, :] = (ADAPTER_SCALE * dot(out_low, oc_ref[0, :, cols], NN)).astype(BF16)
    pairs = [
        ADAPTER_SCALE * dot(low[16:32], dk, NN),
        ADAPTER_SCALE * dot(low[32:48], dv, NN),
    ]
    for s in range(WIDE):
        cols = slice(32 * s, 32 * s + 32)
        out_ref[s, 96:104, :] = jnp.concatenate(
            [pairs[0][:8, cols], pairs[0][8:, cols], pairs[1][:8, cols], pairs[1][8:, cols]], axis=1
        ).astype(BF16)


def grads(mine, x, oc, low, up_out, pairs, *halves):
    return pl.pallas_call(
        grads_kernel,
        out_shape=jax.ShapeDtypeStruct((WIDE, ROWS, 128), BF16),
        in_specs=vmem(14),
        out_specs=pl.BlockSpec(memory_space=pltpu.VMEM),
        compiler_params=pltpu.CompilerParams(vmem_limit_bytes=12 << 20),
        name="grads",
    )(mine, x, oc, low, up_out, pairs, *halves)


def combine_kernel(ids_ref, lane_ref, back_ref, mine_ref, o1_ref, o2_ref, o3_ref, acc_ref):
    acc_ref[...] = jnp.zeros_like(acc_ref)

    def step(n, carry):
        a = ids_ref[0, n]
        acc_ref[a] += back_ref[n].astype(F32)
        return carry

    lax.fori_loop(0, WIDE, step, 0)
    y = lane_ref[4]
    mine_ref[...] = acc_ref[pl.ds(4 * y, 4)]
    for shift, ref in ((1, o1_ref), (2, o2_ref), (3, o3_ref)):
        ref[...] = acc_ref[pl.ds(4 * lax.rem(y + shift, 4), 4)].astype(BF16)


def combine(ids, place, back):
    quarter = (4, ROWS, 128)
    return pl.pallas_call(
        combine_kernel,
        out_shape=(
            jax.ShapeDtypeStruct(quarter, F32),
            jax.ShapeDtypeStruct(quarter, BF16),
            jax.ShapeDtypeStruct(quarter, BF16),
            jax.ShapeDtypeStruct(quarter, BF16),
        ),
        in_specs=[smem(), smem()] + vmem(1),
        out_specs=tuple(vmem(4)),
        scratch_shapes=[pltpu.VMEM((ADAPTERS, ROWS, 128), F32)],
        compiler_params=pltpu.CompilerParams(vmem_limit_bytes=8 << 20),
        name="combine",
    )(ids, place, back)


def quarter_kernel(mine_ref, r1_ref, r2_ref, r3_ref, out_ref):
    value = mine_ref[...]
    for ref in (r1_ref, r2_ref, r3_ref):
        value = value + ref[...].astype(F32)
    out_ref[...] = value.astype(BF16)


def add_kernel(a_ref, b_ref, out_ref):
    out_ref[...] = (a_ref[...].astype(F32) + b_ref[...].astype(F32)).astype(BF16)


def summed(kernel, *terms):
    return pl.pallas_call(
        kernel,
        out_shape=jax.ShapeDtypeStruct(terms[0].shape, BF16),
        in_specs=vmem(len(terms)),
        out_specs=pl.BlockSpec(memory_space=pltpu.VMEM),
        compiler_params=pltpu.CompilerParams(vmem_limit_bytes=4 << 20),
    )(*terms)


def unpack_kernel(lane_ref, q0_ref, q1_ref, q2_ref, q3_ref, down_ref, up_ref, pair_ref):
    y = lane_ref[4]
    for shift, ref in ((0, q0_ref), (1, q1_ref), (2, q2_ref), (3, q3_ref)):
        first = 4 * lax.rem(y + 4 - shift, 4)
        for t in range(4):
            a = first + t
            value = ref[t].astype(F32)
            for p in range(4):
                down_ref[a, p] = value[16 * p : 16 * p + 16]
            for p in range(2):
                up_ref[a, p] = value[64 + 16 * p : 80 + 16 * p]
                for h in range(2):
                    g = 2 * p + h
                    pair_ref[a, p, 8 * h : 8 * h + 8, :] = value[96:104, 32 * g : 32 * g + 32]


def unpack(place, quarters):
    return pl.pallas_call(
        unpack_kernel,
        out_shape=(
            jax.ShapeDtypeStruct((ADAPTERS, 4, RANK, 128), F32),
            jax.ShapeDtypeStruct((ADAPTERS, 2, RANK, 128), F32),
            jax.ShapeDtypeStruct((ADAPTERS, 2, RANK, 32), F32),
        ),
        in_specs=[smem()] + vmem(4),
        out_specs=tuple(vmem(3)),
        compiler_params=pltpu.CompilerParams(vmem_limit_bytes=8 << 20),
        name="unpack",
    )(place, *quarters)


def y_shift(value, shift):
    pairs = [(2 * y + z, 2 * ((y + shift) % 4) + z) for y in range(4) for z in range(2)]
    return lax.ppermute(value, "prompt", pairs)


def z_swap(value):
    return lax.ppermute(value, "prompt", [(p, p ^ 1) for p in range(8)])


def wide_index(x, z, core):
    return (4 * (x % 4) + z % 4) * 2 + core


def wide_move(value, dx, dz, dcore):
    pairs = [
        (wide_index(x, z, c), wide_index(x + dx, z + dz, c ^ dcore))
        for x in range(4) for z in range(4) for c in range(2)
    ]
    return lax.ppermute(value, "wide", pairs)


def gather_part(mine):
    moved = [wide_move(mine, 0, s, 0) for s in (1, 2, 3)]
    column = column_of([mine] + moved)
    return [column] + [wide_move(column, s, 0, 0) for s in (1, 3, 2)]


def step(
    candidate_hidden, frozen_query, candidate_key_value, prompt_key_value, candidate_adapter,
    prompt_block_end, adapter_down, adapter_up, adapter_up_key_value, output_cotangent,
    context_cotangent,
):
    prompts = split_prompt(prompt_key_value)
    sent, place = pack(
        candidate_adapter, prompt_block_end, adapter_down, adapter_up, adapter_up_key_value
    )
    mine = lax.all_to_all(sent, "wide", 0, 0, tiled=True)
    parts = []
    for part in range(2):
        pieces = gather_part(prompts[part])
        parts.append(pieces + [wide_move(piece, 0, 0, 1) for piece in pieces])
    q, own, cg, low, up_out, pairs = prep(
        mine, candidate_hidden, frozen_query, candidate_key_value, output_cotangent,
        context_cotangent,
    )
    halves = []
    for part in range(2):
        halves += attention_call(part, place, q, cg, own, parts[part])
    blocks = grads(mine, candidate_hidden, output_cotangent, low, up_out, pairs, *halves)
    back = lax.all_to_all(blocks, "wide", 0, 0, tiled=True)
    total, *others = combine(candidate_adapter, place, back)
    received = [y_shift(other, shift) for shift, other in zip((1, 2, 3), others)]
    quarter = summed(quarter_kernel, total, *received)
    quarter = summed(add_kernel, quarter, z_swap(quarter))
    quarters = [quarter] + [y_shift(quarter, shift) for shift in (1, 2, 3)]
    return unpack(place, quarters)


def solution(mesh):
    tokens = P("prompt", "wide", None)
    columns = P(None, None, None, "wide")
    placed = (
        tokens, tokens, tokens, tokens, P("prompt", None), P("prompt", "wide"),
        columns, columns, columns, tokens, tokens,
    )
    return jax.shard_map(
        step, mesh=mesh, in_specs=placed, out_specs=(columns, columns, columns), check_vma=False
    )
```

```python
import jax
import jax.numpy as jnp
from jax import lax
from jax.experimental import pallas as pl
from jax.experimental.pallas import tpu as pltpu
from jax.sharding import PartitionSpec as P


KV_HEADS = 8
HEAD_DIM = 128
ADAPTERS = 16
RANK = 16
BLOCK = 128
WIDE = 32
ROWS = 104
ADAPTER_SCALE = 2.0
MASKED = -1e30
INVERSE_ROOT = HEAD_DIM ** (-0.5)
LOG2E = 1.4426950408889634
KEY_CHUNK = 256
SHIFTS = (0, 1, 3, 2)
HALVES = (slice(0, 256), slice(256, 512))

BF16 = jnp.bfloat16
F32 = jnp.float32


def dot(a, b, dims):
    return lax.dot_general(a, b, (dims, ((), ())), preferred_element_type=F32)


NN = ((1,), (0,))
NT = ((1,), (1,))
TN = ((0,), (0,))


def vmem(n):
    return [pl.BlockSpec(memory_space=pltpu.VMEM)] * n


def smem():
    return pl.BlockSpec(memory_space=pltpu.SMEM)


def pack_kernel(ids_ref, end_ref, down_ref, up_ref, pair_ref, out_ref, place_ref, joined_ref):
    lane = lax.axis_index("wide")
    group = lax.axis_index("prompt")
    numbers = (lane // 8, lax.rem(lane // 2, 4), lax.rem(lane, 2), end_ref[0, 0])
    for i, value in enumerate(numbers + (group // 2, lax.rem(group, 2))):
        place_ref[i] = value

    for a in range(ADAPTERS):
        pieces = []
        for p in range(2):
            pair = pair_ref[a, p].astype(F32)
            pieces += [pair[:8], pair[8:]]
        joined_ref[a] = jnp.concatenate(pieces, axis=1)
    for n in range(WIDE):
        a = ids_ref[0, n]
        for p in range(4):
            out_ref[n, 16 * p : 16 * p + 16, :] = down_ref[a, p]
        for p in range(2):
            out_ref[n, 64 + 16 * p : 80 + 16 * p, :] = up_ref[a, p]
        out_ref[n, 96:104, :] = joined_ref[a].astype(BF16)


def pack(ids, end, down, up, pairs):
    return pl.pallas_call(
        pack_kernel,
        out_shape=(
            jax.ShapeDtypeStruct((WIDE, ROWS, 128), BF16),
            jax.ShapeDtypeStruct((8,), jnp.int32),
        ),
        in_specs=[smem(), smem()] + vmem(3),
        out_specs=(pl.BlockSpec(memory_space=pltpu.VMEM), smem()),
        scratch_shapes=[pltpu.VMEM((ADAPTERS, 8, 128), F32)],
        compiler_params=pltpu.CompilerParams(vmem_limit_bytes=4 << 20),
        name="pack",
    )(ids, end, down, up, pairs)


def split_kernel(prompt_ref, first_ref, second_ref):
    for part, ref in enumerate((first_ref, second_ref)):
        ref[:, :512] = prompt_ref[0, :, 512 * part : 512 * part + 512]
        ref[:, 512:] = prompt_ref[0, :, 1024 + 512 * part : 1536 + 512 * part]


def split_prompt(prompt):
    half = jax.ShapeDtypeStruct((64, 1024), BF16)
    return pl.pallas_call(
        split_kernel,
        out_shape=(half, half),
        in_specs=vmem(1),
        out_specs=tuple(vmem(2)),
        compiler_params=pltpu.CompilerParams(vmem_limit_bytes=2 << 20),
        name="split",
    )(prompt)


def column_kernel(a_ref, b_ref, c_ref, d_ref, out_ref):
    for i, ref in enumerate((a_ref, b_ref, c_ref, d_ref)):
        out_ref[i] = ref[...]


def column_of(pieces):
    return pl.pallas_call(
        column_kernel,
        out_shape=jax.ShapeDtypeStruct((4, 64, 1024), BF16),
        in_specs=vmem(4),
        out_specs=pl.BlockSpec(memory_space=pltpu.VMEM),
        compiler_params=pltpu.CompilerParams(vmem_limit_bytes=4 << 20),
        name="column",
    )(*pieces)


def wide_rows(ref, start, stop):
    return jnp.concatenate([ref[s, start:stop, :] for s in range(WIDE)], axis=1)


def pair_rows(ref):
    parts = []
    for g in range(4):
        pieces = []
        for s in range(WIDE):
            pieces.append(ref[s, 96:104, 32 * g : 32 * g + 32].astype(F32))
        parts.append(jnp.concatenate(pieces, axis=1))
    return jnp.concatenate(parts, axis=0).astype(BF16)


def prep_kernel(
    mine_ref, x_ref, fq_ref, ckv_ref, oc_ref, cc_ref,
    q_ref, own_ref, cg_ref, low_ref, upout_ref, pair_ref,
):
    low = dot(wide_rows(mine_ref, 0, 48), x_ref[0], NT).astype(BF16)
    low_ref[...] = low
    up_out = (ADAPTER_SCALE * dot(wide_rows(mine_ref, 80, 96), oc_ref[0], NT)).astype(BF16)
    upout_ref[...] = up_out
    pairs = pair_rows(mine_ref)
    pair_ref[...] = pairs
    for s in range(WIDE):
        cols = slice(128 * s, 128 * s + 128)
        delta = dot(low[:16], mine_ref[s, 64:80, :], TN)
        q_ref[:, cols] = (fq_ref[0, :, cols].astype(F32) + ADAPTER_SCALE * delta).astype(BF16)
        delta = dot(up_out, mine_ref[s, 48:64, :], TN)
        cg_ref[:, cols] = (cc_ref[0, :, cols].astype(F32) + delta).astype(BF16)
    for h in range(2):
        cols = slice(1024 * h, 1024 * h + 1024)
        delta = dot(low[16 + 16 * h : 32 + 16 * h], pairs[16 * h : 16 * h + 16], TN)
        own_ref[:, cols] = (ckv_ref[0, :, cols].astype(F32) + ADAPTER_SCALE * delta).astype(BF16)


def prep(mine, x, fq, ckv, oc, cc):
    return pl.pallas_call(
        prep_kernel,
        out_shape=(
            jax.ShapeDtypeStruct((BLOCK, 4096), BF16),
            jax.ShapeDtypeStruct((BLOCK, 2048), BF16),
            jax.ShapeDtypeStruct((BLOCK, 4096), BF16),
            jax.ShapeDtypeStruct((48, 128), BF16),
            jax.ShapeDtypeStruct((16, 128), BF16),
            jax.ShapeDtypeStruct((32, 1024), BF16),
        ),
        in_specs=vmem(6),
        out_specs=tuple(vmem(6)),
        compiler_params=pltpu.CompilerParams(vmem_limit_bytes=12 << 20),
        name="prep",
    )(mine, x, fq, ckv, oc, cc)


def stack_heads(ref):
    return jnp.concatenate([ref[:, 128 * g : 128 * g + 128] for g in range(4)], axis=0)


def piece_mask(limit_ref, shift, other):
    x, z, core, end = (limit_ref[i] for i in range(4))
    side = core ^ other
    lane = lax.broadcasted_iota(jnp.int32, (1, KEY_CHUNK), 1)
    origin = jnp.zeros((1, KEY_CHUNK), jnp.int32)
    for t in range(4):
        source = (lax.rem(x + 4 - shift, 4) * 4 + lax.rem(z + 4 - t, 4)) * 2 + side
        origin = jnp.where(lane >= 64 * t, source, origin)
    return origin < 2 * end


def attention_kernel(
    limit_ref, q_ref, cg_ref, ok_ref, ov_ref, *refs,
):
    k_refs, v_refs = refs[:8], refs[8:16]
    ctx_ref, dq_ref, dk_ref, dv_ref, s_ref, p_ref = refs[16:]
    factor = INVERSE_ROOT * LOG2E
    q4 = stack_heads(q_ref)
    cg4 = stack_heads(cg_ref)
    own_k = ok_ref[...]
    own_v = ov_ref[...]
    row = lax.broadcasted_iota(jnp.int32, (512, BLOCK), 0) & (BLOCK - 1)
    col = lax.broadcasted_iota(jnp.int32, (512, BLOCK), 1)
    own_s = jnp.where(col <= row, dot(q4, own_k, NT), MASKED)
    peak = own_s
    for j in range(8):
        rows = slice(KEY_CHUNK * j, KEY_CHUNK * (j + 1))
        s = dot(q4, k_refs[j][...].reshape(KEY_CHUNK, 128), NT)
        s = jnp.where(piece_mask(limit_ref, SHIFTS[j % 4], j // 4), s, MASKED)
        s_ref[:, rows] = s
        for t in range(KEY_CHUNK // 128):
            peak = jnp.maximum(peak, s[:, 128 * t : 128 * t + 128])
    peak = jnp.max(peak, axis=1, keepdims=True) * factor
    own_p = jnp.exp2(own_s * factor - peak)
    total = own_p
    own_p16 = own_p.astype(BF16)
    weighted = [dot(own_p16[r], own_v, NN) for r in HALVES]
    for j in range(8):
        rows = slice(KEY_CHUNK * j, KEY_CHUNK * (j + 1))
        p = jnp.exp2(s_ref[:, rows] * factor - peak)
        for t in range(KEY_CHUNK // 128):
            total = total + p[:, 128 * t : 128 * t + 128]
        p16 = p.astype(BF16)
        p_ref[:, rows] = p16
        value = v_refs[j][...].reshape(KEY_CHUNK, 128)
        weighted = [w + dot(p16[r], value, NN) for w, r in zip(weighted, HALVES)]
    total = jnp.sum(total, axis=1, keepdims=True)
    context = (jnp.concatenate(weighted, axis=0) / total).astype(BF16)
    delta = jnp.sum(cg4.astype(F32) * context.astype(F32), axis=1, keepdims=True)
    attention = own_p / total
    own_ds = (attention * (dot(cg4, own_v, NT) - delta)).astype(BF16)
    grad = [jnp.zeros((256, 128), F32)] * 2
    for j in range(8):
        rows = slice(KEY_CHUNK * j, KEY_CHUNK * (j + 1))
        dp = dot(cg4, v_refs[j][...].reshape(KEY_CHUNK, 128), NT)
        ds = (p_ref[:, rows].astype(F32) * (dp - delta)).astype(BF16)
        key = k_refs[j][...].reshape(KEY_CHUNK, 128)
        grad = [w + dot(ds[r], key, NN) for w, r in zip(grad, HALVES)]
    grad = (jnp.concatenate(grad, axis=0) / total + dot(own_ds, own_k, NN)) * INVERSE_ROOT
    grad = grad.astype(BF16)
    for g in range(4):
        ctx_ref[:, 128 * g : 128 * g + 128] = context[128 * g : 128 * g + 128]
        dq_ref[:, 128 * g : 128 * g + 128] = grad[128 * g : 128 * g + 128]
    dk_ref[...] = (dot(own_ds, q4, TN) * INVERSE_ROOT).astype(BF16)
    dv_ref[...] = dot(attention.astype(BF16), cg4, TN).astype(BF16)


def attention_call(part, place, q, cg, own, pieces):
    first = 4 * part
    heads_in = pl.BlockSpec((BLOCK, 512), lambda k: (0, k + first))
    heads = pl.BlockSpec((BLOCK, 512), lambda k: (0, k))
    head = pl.BlockSpec((BLOCK, 128), lambda k: (0, k))
    return pl.pallas_call(
        attention_kernel,
        grid=(4,),
        out_shape=(
            jax.ShapeDtypeStruct((BLOCK, 2048), BF16),
            jax.ShapeDtypeStruct((BLOCK, 2048), BF16),
            jax.ShapeDtypeStruct((BLOCK, 512), BF16),
            jax.ShapeDtypeStruct((BLOCK, 512), BF16),
        ),
        in_specs=[
            smem(),
            heads_in,
            heads_in,
            pl.BlockSpec((BLOCK, 128), lambda k: (0, k + first)),
            pl.BlockSpec((BLOCK, 128), lambda k: (0, k + first + KV_HEADS)),
        ]
        + [pl.BlockSpec((4, 64, 128), lambda k: (0, 0, k))] * 8
        + [pl.BlockSpec((4, 64, 128), lambda k: (0, 0, k + 4))] * 8,
        out_specs=(heads, heads, head, head),
        scratch_shapes=[
            pltpu.VMEM((512, 2048), F32),
            pltpu.VMEM((512, 2048), BF16),
        ],
        compiler_params=pltpu.CompilerParams(
            dimension_semantics=("arbitrary",), vmem_limit_bytes=18 << 20
        ),
        cost_estimate=pl.CostEstimate(
            flops=12_000_000_000, bytes_accessed=8_000_000, transcendentals=4_000_000
        ),
    )(place, q, cg, own, own, *pieces, *pieces)


def grads_kernel(
    mine_ref, x_ref, oc_ref, low_ref, upout_ref, pair_ref,
    *refs,
):
    out_ref = refs[8]
    low = low_ref[...]
    context, dq, dk, dv = (
        jnp.concatenate([refs[i][...], refs[i + 4][...]], axis=1) for i in range(4)
    )
    out_low = dot(wide_rows(mine_ref, 48, 64), context, NT).astype(BF16)
    up_q = (ADAPTER_SCALE * dot(wide_rows(mine_ref, 64, 80), dq, NT)).astype(BF16)
    up_k = (ADAPTER_SCALE * dot(pair_ref[:16], dk, NT)).astype(BF16)
    up_v = (ADAPTER_SCALE * dot(pair_ref[16:], dv, NT)).astype(BF16)
    up_low = jnp.concatenate([up_q, up_k, up_v], axis=0)
    up_out = upout_ref[...]
    for s in range(WIDE):
        cols = slice(128 * s, 128 * s + 128)
        out_ref[s, 0:48, :] = dot(up_low, x_ref[0, :, cols], NN).astype(BF16)
        out_ref[s, 48:64, :] = dot(up_out, context[:, cols], NN).astype(BF16)
        out_ref[s, 64:80, :] = (ADAPTER_SCALE * dot(low[:16], dq[:, cols], NN)).astype(BF16)
        out_ref[s, 80:96, :] = (ADAPTER_SCALE * dot(out_low, oc_ref[0, :, cols], NN)).astype(BF16)
    pairs = [
        ADAPTER_SCALE * dot(low[16:32], dk, NN),
        ADAPTER_SCALE * dot(low[32:48], dv, NN),
    ]
    for s in range(WIDE):
        cols = slice(32 * s, 32 * s + 32)
        out_ref[s, 96:104, :] = jnp.concatenate(
            [pairs[0][:8, cols], pairs[0][8:, cols], pairs[1][:8, cols], pairs[1][8:, cols]], axis=1
        ).astype(BF16)


def grads(mine, x, oc, low, up_out, pairs, *halves):
    return pl.pallas_call(
        grads_kernel,
        out_shape=jax.ShapeDtypeStruct((WIDE, ROWS, 128), BF16),
        in_specs=vmem(14),
        out_specs=pl.BlockSpec(memory_space=pltpu.VMEM),
        compiler_params=pltpu.CompilerParams(vmem_limit_bytes=12 << 20),
        name="grads",
    )(mine, x, oc, low, up_out, pairs, *halves)


def combine_kernel(ids_ref, lane_ref, back_ref, mine_ref, o1_ref, o2_ref, o3_ref, acc_ref):
    acc_ref[...] = jnp.zeros_like(acc_ref)

    def step(n, carry):
        a = ids_ref[0, n]
        acc_ref[a] += back_ref[n].astype(F32)
        return carry

    lax.fori_loop(0, WIDE, step, 0)
    y = lane_ref[4]
    mine_ref[...] = acc_ref[pl.ds(4 * y, 4)]
    for shift, ref in ((1, o1_ref), (2, o2_ref), (3, o3_ref)):
        ref[...] = acc_ref[pl.ds(4 * lax.rem(y + shift, 4), 4)].astype(BF16)


def combine(ids, place, back):
    quarter = (4, ROWS, 128)
    return pl.pallas_call(
        combine_kernel,
        out_shape=(
            jax.ShapeDtypeStruct(quarter, F32),
            jax.ShapeDtypeStruct(quarter, BF16),
            jax.ShapeDtypeStruct(quarter, BF16),
            jax.ShapeDtypeStruct(quarter, BF16),
        ),
        in_specs=[smem(), smem()] + vmem(1),
        out_specs=tuple(vmem(4)),
        scratch_shapes=[pltpu.VMEM((ADAPTERS, ROWS, 128), F32)],
        compiler_params=pltpu.CompilerParams(vmem_limit_bytes=8 << 20),
        name="combine",
    )(ids, place, back)


def quarter_kernel(mine_ref, r1_ref, r2_ref, r3_ref, out_ref):
    value = mine_ref[...]
    for ref in (r1_ref, r2_ref, r3_ref):
        value = value + ref[...].astype(F32)
    out_ref[...] = value.astype(BF16)


def add_kernel(a_ref, b_ref, out_ref):
    out_ref[...] = (a_ref[...].astype(F32) + b_ref[...].astype(F32)).astype(BF16)


def summed(kernel, *terms):
    return pl.pallas_call(
        kernel,
        out_shape=jax.ShapeDtypeStruct(terms[0].shape, BF16),
        in_specs=vmem(len(terms)),
        out_specs=pl.BlockSpec(memory_space=pltpu.VMEM),
        compiler_params=pltpu.CompilerParams(vmem_limit_bytes=4 << 20),
    )(*terms)


def unpack_kernel(lane_ref, q0_ref, q1_ref, q2_ref, q3_ref, down_ref, up_ref, pair_ref):
    y = lane_ref[4]
    for shift, ref in ((0, q0_ref), (1, q1_ref), (2, q2_ref), (3, q3_ref)):
        first = 4 * lax.rem(y + 4 - shift, 4)
        for t in range(4):
            a = first + t
            value = ref[t].astype(F32)
            for p in range(4):
                down_ref[a, p] = value[16 * p : 16 * p + 16]
            for p in range(2):
                up_ref[a, p] = value[64 + 16 * p : 80 + 16 * p]
                for h in range(2):
                    g = 2 * p + h
                    pair_ref[a, p, 8 * h : 8 * h + 8, :] = value[96:104, 32 * g : 32 * g + 32]


def unpack(place, quarters):
    return pl.pallas_call(
        unpack_kernel,
        out_shape=(
            jax.ShapeDtypeStruct((ADAPTERS, 4, RANK, 128), F32),
            jax.ShapeDtypeStruct((ADAPTERS, 2, RANK, 128), F32),
            jax.ShapeDtypeStruct((ADAPTERS, 2, RANK, 32), F32),
        ),
        in_specs=[smem()] + vmem(4),
        out_specs=tuple(vmem(3)),
        compiler_params=pltpu.CompilerParams(vmem_limit_bytes=8 << 20),
        name="unpack",
    )(place, *quarters)


def y_shift(value, shift):
    pairs = [(2 * y + z, 2 * ((y + shift) % 4) + z) for y in range(4) for z in range(2)]
    return lax.ppermute(value, "prompt", pairs)


def z_swap(value):
    return lax.ppermute(value, "prompt", [(p, p ^ 1) for p in range(8)])


def wide_index(x, z, core):
    return (4 * (x % 4) + z % 4) * 2 + core


def wide_move(value, dx, dz, dcore):
    pairs = [
        (wide_index(x, z, c), wide_index(x + dx, z + dz, c ^ dcore))
        for x in range(4) for z in range(4) for c in range(2)
    ]
    return lax.ppermute(value, "wide", pairs)


def gather_part(mine, part):
    moved = [wide_move(mine, 0, s, 0) for s in (1, 2, 3)]
    column = jnp.stack([mine] + moved) if part else column_of([mine] + moved)
    return [column] + [wide_move(column, s, 0, 0) for s in (1, 3, 2)]


def step(
    candidate_hidden, frozen_query, candidate_key_value, prompt_key_value, candidate_adapter,
    prompt_block_end, adapter_down, adapter_up, adapter_up_key_value, output_cotangent,
    context_cotangent,
):
    prompts = split_prompt(prompt_key_value)
    sent, place = pack(
        candidate_adapter, prompt_block_end, adapter_down, adapter_up, adapter_up_key_value
    )
    mine = lax.all_to_all(sent, "wide", 0, 0, tiled=True)
    parts = []
    for part in range(2):
        pieces = gather_part(prompts[part], part)
        parts.append(pieces + [wide_move(piece, 0, 0, 1) for piece in pieces])
    q, own, cg, low, up_out, pairs = prep(
        mine, candidate_hidden, frozen_query, candidate_key_value, output_cotangent,
        context_cotangent,
    )
    halves = []
    for part in range(2):
        halves += attention_call(part, place, q, cg, own, parts[part])
    blocks = grads(mine, candidate_hidden, output_cotangent, low, up_out, pairs, *halves)
    back = lax.all_to_all(blocks, "wide", 0, 0, tiled=True)
    total, *others = combine(candidate_adapter, place, back)
    received = [y_shift(other, shift) for shift, other in zip((1, 2, 3), others)]
    quarter = summed(quarter_kernel, total, *received)
    quarter = summed(add_kernel, quarter, z_swap(quarter))
    quarters = [quarter] + [y_shift(quarter, shift) for shift in (1, 2, 3)]
    return unpack(place, quarters)


def solution(mesh):
    tokens = P("prompt", "wide", None)
    columns = P(None, None, None, "wide")
    placed = (
        tokens, tokens, tokens, tokens, P("prompt", None), P("prompt", "wide"),
        columns, columns, columns, tokens, tokens,
    )
    return jax.shard_map(
        step, mesh=mesh, in_specs=placed, out_specs=(columns, columns, columns), check_vma=False
    )
```
